32 devices in a mesh: group: 2 (over y), tm: 16 (over z, x, core), height: 1.
Axes of the slice: x: 2, y: 2, z: 4, core: 2. Of those that a mesh axis runs over, the one named last changes fastest.
Arguments:
- query: bfloat16 [32, 2, 64, 1536], P(('group', 'tm'), 'height'), parts along dimension 0
- cur_kv: bfloat16 [2, 32, 2, 64, 1536], P(None, ('group', 'tm'), 'height'), parts along dimension 1
- cur_pos: int32 [3, 32, 2, 64], P(None, ('group', 'tm'), 'height'), parts along dimension 1, may hold values from 0 to 63
- cache_kv: bfloat16 [32, 2, 32, 1536], P(('group', 'tm'), None, 'height'), parts along dimension 0
- cache_pos: int32 [32, 3, 32], P(('group', 'tm'), None, 'height'), parts along dimension 0, may hold values from 0 to 63
- counts: int32 [32, 1], P(('group', 'tm'), 'height'), parts along dimension 0, may hold values from 1 to 32
- visible: int32 [32, 16], P(('group', 'tm')), parts along dimension 0, may hold values 0 or 1
Outputs:
- attended: bfloat16 [32, 2, 64, 1536], P(('group', 'tm'), 'height'), parts along dimension 0
The draws below stay inside these ranges and needn't reach their ends.
There are 2 independent parts, one for each index of `group`. The reference program is written for one: setup_inputs(seed, part) draws one part's arguments, and reference() takes and returns one part's arrays. A program takes and returns all parts, laid end to end along the dimension named above; each array names one. Nothing has to cross between parts.
Inputs may be any that keep to these rules, and one draw needn't show every extreme that they name: `counts`: every earlier span has at least one live slot in each row tile.
All inputs are finite; a program needn't handle non-finite values. No bound on the sum of `visible` on one device may be relied on, other than what follows from the above.
Results may differ from the reference program's by a relative error of at most 0.006.
The reference program's roundings to bfloat16 on the way count: a program that leaves them out, or rounds other values in their place, can miss the bound.
Values may be sent and summed in bfloat16 or wider, within the bound.
A program may use at most 64 MiB of HBM per device.

```python
import jax
import jax.numpy as jnp
from jax import lax

HEADS = 12
HEAD = 128
ROWS_DEV = 2
WID = 64
CTOK = 32
REACH = 2
NROWS = 2
SPAN_FR = 16
CACHED = 16
HT_TOK = 32
N_HEIGHT = 1


def draw_tokens(key, shape):
    base = jnp.clip(jax.random.normal(key, shape, jnp.float32), -4.0, 4.0)
    return base.astype(jnp.bfloat16)


def draw_query(key, part):
    return draw_tokens(jax.random.fold_in(key, 11), (SPAN_FR, NROWS, WID, HEADS * HEAD))


def draw_cur_kv(key, part):
    return draw_tokens(jax.random.fold_in(key, 13), (2, SPAN_FR, NROWS, WID, HEADS * HEAD))


def draw_cache_kv(key, part):
    return draw_tokens(jax.random.fold_in(key, 17), (CACHED, 2, HT_TOK, HEADS * HEAD))


def plant(drawn, rng, least, largest):
    spot = [jax.random.randint(jax.random.fold_in(rng, axis), (), 0, length) for axis, length in enumerate(drawn.shape)]
    widest = drawn.shape.index(max(drawn.shape))
    beside = spot[:widest] + [(spot[widest] + 1) % drawn.shape[widest]] + spot[widest + 1:]
    return drawn.at[tuple(spot)].set(least).at[tuple(beside)].set(largest)


def setup_inputs(seed: int = 0, part: int = 0) -> dict:
    arg_keys = jax.random.split(jax.random.key(seed), 8)
    part_keys = jax.random.split(jax.random.fold_in(arg_keys[7], part), 8)
    return {
        "query": draw_query(jax.random.fold_in(jax.random.fold_in(arg_keys[7], part), 71), part),
        "cur_kv": draw_cur_kv(jax.random.fold_in(jax.random.fold_in(arg_keys[7], part), 71), part),
        "cur_pos": plant(jax.random.randint(part_keys[2], (3, SPAN_FR, NROWS, WID), 0, 64), jax.random.fold_in(part_keys[2], 1), 0, 63).astype(jnp.int32),
        "cache_kv": draw_cache_kv(jax.random.fold_in(jax.random.fold_in(arg_keys[7], part), 71), part),
        "cache_pos": plant(jax.random.randint(part_keys[4], (CACHED, 3, HT_TOK), 0, 64), jax.random.fold_in(part_keys[4], 1), 0, 63).astype(jnp.int32),
        "counts": plant(jax.random.randint(part_keys[5], (CACHED, N_HEIGHT), 1, CTOK + 1), jax.random.fold_in(part_keys[5], 1), 1, CTOK).astype(jnp.int32),
        "visible": plant((jax.random.randint(part_keys[6], (SPAN_FR, CACHED), 0, 4) < 3).astype(jnp.int32), jax.random.fold_in(part_keys[6], 1), 0, 1),
    }


def rope_tables():
    half = HEAD // 2
    index = jnp.arange(half)
    first = HEAD // 8
    second = 3 * HEAD // 16
    member = (index >= first).astype(jnp.int32) + (index >= first + second).astype(jnp.int32)
    begin = jnp.where(member == 0, 0, jnp.where(member == 1, first, first + second))
    length = jnp.where(member == 0, first, jnp.where(member == 1, second, half - first - second))
    frequency = jnp.power(10000.0, -(index - begin).astype(jnp.float32) / length.astype(jnp.float32))
    select = (member[None, :] == jnp.arange(3)[:, None]).astype(jnp.float32) * frequency[None, :]
    return select


def rotate(vectors, pos_time, pos_row, pos_column):
    select = rope_tables()
    angle = (pos_time.astype(jnp.float32)[..., None] * select[0]
             + pos_row.astype(jnp.float32)[..., None] * select[1]
             + pos_column.astype(jnp.float32)[..., None] * select[2])
    cosine = jnp.cos(angle)[..., None, :]
    sine = jnp.sin(angle)[..., None, :]
    shaped = vectors.astype(jnp.float32).reshape(vectors.shape[:-1] + (HEADS, 2, HEAD // 2))
    lower = shaped[..., 0, :]
    upper = shaped[..., 1, :]
    turned = jnp.stack([lower * cosine - upper * sine, upper * cosine + lower * sine], axis=-2)
    return turned.reshape(vectors.shape).astype(jnp.bfloat16)


def reference(query, cur_kv, cur_pos, cache_kv, cache_pos, counts, visible):
    depth = HEADS * HEAD
    scale = HEAD ** -0.5
    q_rot = rotate(query, cur_pos[0], cur_pos[1], cur_pos[2])
    k_rot = rotate(cur_kv[0], cur_pos[0], cur_pos[1], cur_pos[2])
    c_rot = rotate(cache_kv[:, 0], cache_pos[:, 0], cache_pos[:, 1], cache_pos[:, 2])
    c_values = cache_kv[:, 1]
    zero_rows = jnp.zeros((SPAN_FR, REACH, WID, depth), jnp.bfloat16)
    k_padded = jnp.concatenate([zero_rows, k_rot, zero_rows], axis=1)
    v_padded = jnp.concatenate([zero_rows, cur_kv[1], zero_rows], axis=1)
    extent = ROWS_DEV + 2 * REACH
    queries = ROWS_DEV * WID

    def one_tile(number):
        frame = (number // N_HEIGHT).astype(jnp.int32)
        tile_row = (number % N_HEIGHT).astype(jnp.int32)
        first_row = tile_row * ROWS_DEV
        zero = jnp.zeros((), jnp.int32)
        q_tile = lax.dynamic_slice(q_rot, (frame, first_row, zero, zero), (1, ROWS_DEV, WID, depth)).reshape(queries, HEADS, HEAD)
        k_tile = lax.dynamic_slice(k_padded, (frame, first_row, zero, zero), (1, extent, WID, depth)).reshape(extent * WID, HEADS, HEAD)
        v_tile = lax.dynamic_slice(v_padded, (frame, first_row, zero, zero), (1, extent, WID, depth)).reshape(extent * WID, HEADS, HEAD)
        c_keys = lax.dynamic_slice(c_rot, (zero, tile_row * CTOK, zero), (CACHED, CTOK, depth)).reshape(CACHED * CTOK, HEADS, HEAD)
        c_vals = lax.dynamic_slice(c_values, (zero, tile_row * CTOK, zero), (CACHED, CTOK, depth)).reshape(CACHED * CTOK, HEADS, HEAD)
        all_keys = jnp.concatenate([k_tile, c_keys], axis=0)
        all_values = jnp.concatenate([v_tile, c_vals], axis=0)
        query_row = first_row + jnp.arange(queries) // WID
        key_row = first_row - REACH + jnp.arange(extent * WID) // WID
        local_ok = ((key_row[None, :] >= 0) & (key_row[None, :] < NROWS)
                    & (jnp.abs(query_row[:, None] - key_row[None, :]) <= REACH))
        live = lax.dynamic_slice(counts, (zero, tile_row), (CACHED, 1))[:, 0]
        seen = lax.dynamic_slice(visible, (frame, zero), (1, CACHED))[0]
        cache_ok = ((seen[:, None] > 0) & (jnp.arange(CTOK)[None, :] < live[:, None])).reshape(CACHED * CTOK)
        allowed = jnp.concatenate([local_ok, jnp.broadcast_to(cache_ok[None, :], (queries, CACHED * CTOK))], axis=1)
        scores = jnp.einsum("qhd,khd->qhk", q_tile.astype(jnp.float32), all_keys.astype(jnp.float32)) * scale
        scores = jnp.where(allowed[:, None, :], scores, -jnp.inf)
        highest = jnp.max(scores, axis=-1, keepdims=True)
        weights = jnp.where(allowed[:, None, :], jnp.exp(scores - highest), 0.0)
        totals = jnp.sum(weights, axis=-1)
        rounded = lax.optimization_barrier(weights.astype(jnp.bfloat16))
        summed = jnp.einsum("qhk,khd->qhd", rounded.astype(jnp.float32), all_values.astype(jnp.float32))
        return (summed / totals[..., None]).astype(jnp.bfloat16).reshape(ROWS_DEV, WID, depth)

    tiles = lax.map(one_tile, jnp.arange(SPAN_FR * N_HEIGHT))
    return tiles.reshape(SPAN_FR, NROWS, WID, depth)
```

```python
import jax
import jax.numpy as jnp
from jax import lax
from jax.experimental import pallas as pl
from jax.experimental.pallas import tpu as pltpu
from jax.sharding import PartitionSpec as P

HEADS = 12
HEAD = 128
REACH = 2


masked_value = -1e30


def extended(cells, sides, width):
    for axis, dim in sides:
        count = lax.axis_size(axis)
        ends = count - 1
        head = lax.slice_in_dim(cells, 0, width, axis=dim)
        tail = lax.slice_in_dim(cells, cells.shape[dim] - width, cells.shape[dim], axis=dim)
        cells = jnp.concatenate(
            [
                lax.ppermute(tail, axis, [(i, (i + 1) % count) for i in range(ends)]),
                cells,
                lax.ppermute(head, axis, [((i + 1) % count, i) for i in range(ends)]),
            ],
            axis=dim,
        )
    return cells


def rope_tables():
    half = HEAD // 2
    index = jnp.arange(half)
    first = HEAD // 8
    second = 3 * HEAD // 16
    member = (index >= first).astype(jnp.int32) + (index >= first + second).astype(jnp.int32)
    begin = jnp.where(member == 0, 0, jnp.where(member == 1, first, first + second))
    length = jnp.where(member == 0, first, jnp.where(member == 1, second, half - first - second))
    frequency = jnp.power(
        10000.0, -(index - begin).astype(jnp.float32) / length.astype(jnp.float32)
    )
    select = (member[None, :] == jnp.arange(3)[:, None]).astype(jnp.float32) * frequency[None, :]
    return select


def rotate(vectors, pos_time, pos_row, pos_column):
    select = rope_tables()
    angle = (
        pos_time.astype(jnp.float32)[..., None] * select[0]
        + pos_row.astype(jnp.float32)[..., None] * select[1]
        + pos_column.astype(jnp.float32)[..., None] * select[2]
    )
    cosine = jnp.cos(angle)[..., None, :]
    sine = jnp.sin(angle)[..., None, :]
    shaped = vectors.astype(jnp.float32).reshape(vectors.shape[:-1] + (HEADS, 2, HEAD // 2))
    lower = shaped[..., 0, :]
    upper = shaped[..., 1, :]
    turned = jnp.stack([lower * cosine - upper * sine, upper * cosine + lower * sine], axis=-2)
    return turned.reshape(vectors.shape).astype(jnp.bfloat16)


def per_device(query, cur_kv, cur_pos, cache_kv, cache_pos, counts, visible):
    frames, tile_rows, columns, depth = query.shape
    queries = tile_rows * columns
    scale = HEAD ** (-0.5)
    tile_index = lax.axis_index("height")
    frame_rows = tile_rows * lax.axis_size("height")
    q_rot = rotate(query, cur_pos[0], cur_pos[1], cur_pos[2]).reshape(frames, queries, HEADS, HEAD)
    q_heads = jnp.transpose(q_rot, (0, 2, 1, 3))
    k_rot = rotate(cur_kv[0], cur_pos[0], cur_pos[1], cur_pos[2])
    local_pair = jnp.stack([k_rot, cur_kv[1]])
    padded = extended(local_pair, (("height", 2),), REACH)
    extent = tile_rows + 2 * REACH
    local_keys = jnp.transpose(
        padded[0].reshape(frames, extent * columns, HEADS, HEAD), (0, 2, 1, 3)
    )
    local_values = jnp.transpose(
        padded[1].reshape(frames, extent * columns, HEADS, HEAD), (0, 2, 1, 3)
    )
    query_row = tile_index * tile_rows + jnp.arange(queries) // columns
    key_row = tile_index * tile_rows - REACH + jnp.arange(extent * columns) // columns
    local_ok = (
        (key_row[None, :] >= 0)
        & (key_row[None, :] < frame_rows)
        & (jnp.abs(query_row[:, None] - key_row[None, :]) <= REACH)
    )
    local_bias = jnp.where(local_ok, 0.0, masked_value).astype(jnp.float32)
    scores = (
        jnp.einsum("fhqd,fhkd->fhqk", q_heads, local_keys, preferred_element_type=jnp.float32)
        * scale
        + local_bias[None, None]
    )
    highest = jnp.max(scores, axis=-1)
    weights = jnp.exp(scores - highest[..., None])
    totals = jnp.sum(weights, axis=-1)
    summed = jnp.einsum(
        "fhqk,fhkd->fhqd",
        weights.astype(jnp.bfloat16),
        local_values,
        preferred_element_type=jnp.float32,
    )
    slots = cache_kv.shape[2]
    slot_index = jnp.arange(slots)
    pair_piece = lax.all_gather(cache_kv, "tm", axis=0, tiled=True)
    position_piece = lax.all_gather(cache_pos, "tm", axis=0, tiled=True)
    count_piece = lax.all_gather(counts, "tm", axis=0, tiled=True)
    turned = rotate(
        pair_piece[:, 0], position_piece[:, 0], position_piece[:, 1], position_piece[:, 2]
    )
    blocks = turned.shape[0]
    live = count_piece[:, 0]
    usable = (
        (visible[:, :, None] > 0) & (slot_index[None, None, :] < live[None, :, None])
    ).reshape(frames, blocks * slots)
    block_bias = jnp.where(usable, 0.0, masked_value).astype(jnp.float32)
    flat_keys = jnp.transpose(turned.reshape(blocks * slots, HEADS, HEAD), (1, 0, 2))
    flat_values = jnp.transpose(pair_piece[:, 1].reshape(blocks * slots, HEADS, HEAD), (1, 0, 2))
    block_scores = (
        jnp.einsum("fhqd,hkd->fhqk", q_heads, flat_keys, preferred_element_type=jnp.float32) * scale
        + block_bias[:, None, None, :]
    )
    new_max = jnp.maximum(highest, jnp.max(block_scores, axis=-1))
    block_weights = jnp.exp(block_scores - new_max[..., None])
    fading = jnp.exp(highest - new_max)
    added = jnp.einsum(
        "fhqk,hkd->fhqd",
        block_weights.astype(jnp.bfloat16),
        flat_values,
        preferred_element_type=jnp.float32,
    )
    final_total = totals * fading + jnp.sum(block_weights, axis=-1)
    final_sum = summed * fading[..., None] + added
    output = (final_sum / final_total[..., None]).astype(jnp.bfloat16)
    output = jnp.transpose(output, (0, 2, 1, 3))
    return output.reshape(frames, tile_rows, columns, depth)


CORES = 2
COLUMNS = 2
LANE = CORES * COLUMNS
DIRECTIONS = 4


def frequency_rows(axis, shape):
    half = HEAD // 2
    index = lax.broadcasted_iota(jnp.int32, shape, axis) % half
    first = HEAD // 8
    second = 3 * HEAD // 16
    member = (index >= first).astype(jnp.int32) + (index >= first + second).astype(jnp.int32)
    begin = jnp.where(member == 0, 0, jnp.where(member == 1, first, first + second))
    length = jnp.where(member == 0, first, jnp.where(member == 1, second, half - first - second))
    ratio = (index - begin).astype(jnp.float32) / length.astype(jnp.float32)
    return member, jnp.exp(-ratio * 9.210340371976184)


def turn_tables(pos_time, pos_row, pos_column):
    tokens = pos_time.shape[-1]
    member, _ = frequency_rows(0, (HEAD, tokens))
    chosen = jnp.where(member == 0, pos_time, jnp.where(member == 1, pos_row, pos_column))
    eye = (
        lax.broadcasted_iota(jnp.int32, (tokens, tokens), 0)
        == lax.broadcasted_iota(jnp.int32, (tokens, tokens), 1)
    ).astype(jnp.float32).astype(jnp.bfloat16)
    spread = lax.dot_general(
        eye,
        chosen.astype(jnp.float32).astype(jnp.bfloat16),
        (((1,), (1,)), ((), ())),
        preferred_element_type=jnp.float32,
    )
    _, frequency = frequency_rows(1, (1, HEAD))
    angle = spread * frequency
    lane = lax.broadcasted_iota(jnp.int32, (tokens, HEAD), 1)
    sine = jnp.sin(angle)
    return jnp.cos(angle), jnp.where(lane < HEAD // 2, -sine, sine)


def turn(vectors, cosine, sine):
    wide = vectors.astype(jnp.float32)
    return (wide * cosine + pltpu.roll(wide, HEAD // 2, 1) * sine).astype(jnp.bfloat16)


def head_columns(h):
    return slice(h * HEAD, (h + 1) * HEAD)


def span_kernel(
    deep, q_hbm, kv_hbm, cur_pos_ref, cache_ref, cache_pos_ref, count_ref, visible_ref, out_ref,
    q_raw, kv_raw, q_rot, k_rot, cos_ref, sin_ref, keys, values, bias_ref, load_sem, own_sem,
    send_sem, recv_sem,
):
    me = lax.axis_index("tm")
    place = me // LANE
    column = (me % LANE) // CORES
    core = me % CORES
    slots = cache_ref.shape[1]
    depth = cache_ref.shape[2]
    blocks = deep * LANE
    scale = HEAD ** (-0.5)
    core_other = me + 1 - 2 * core
    column_other = me + CORES - 2 * CORES * column
    barrier = pltpu.get_barrier_semaphore()

    def greet(device):
        pl.semaphore_signal(
            barrier, inc=1, device_id={"tm": device}, device_id_type=pl.DeviceIdType.MESH
        )

    greet(core_other)
    greet(column_other)
    pl.when(place > 0)(lambda: greet(me - LANE))
    pl.when(place < deep - 1)(lambda: greet(me + LANE))

    load_q = pltpu.make_async_copy(q_hbm, q_raw, load_sem.at[0])
    load_kv = pltpu.make_async_copy(kv_hbm, kv_raw, load_sem.at[1])
    own_values = pltpu.make_async_copy(cache_ref.at[1], values.at[me], own_sem)
    load_q.start()
    load_kv.start()
    own_values.start()

    cosine, sine = turn_tables(cache_pos_ref[0:1, :], cache_pos_ref[1:2, :], cache_pos_ref[2:3, :])
    for h in range(HEADS):
        keys[me, :, head_columns(h)] = turn(cache_ref[0, :, head_columns(h)], cosine, sine)
    row = lax.broadcasted_iota(jnp.int32, (slots, HEAD), 0)
    keys[me, :, depth:] = jnp.where(row < count_ref[0, 0], 0.0, masked_value).astype(jnp.bfloat16)

    pl.semaphore_wait(
        barrier,
        2 + (place > 0).astype(jnp.int32) + (place < deep - 1).astype(jnp.int32),
    )

    def message(part, slot, direction, device, own=False):
        buffer = (values, keys)[part]
        source = cache_ref.at[1] if own and part == 0 else buffer.at[slot]
        return pltpu.make_async_remote_copy(
            src_ref=source,
            dst_ref=buffer.at[slot],
            send_sem=send_sem.at[part, slot, direction],
            recv_sem=recv_sem.at[part, slot],
            device_id={"tm": device},
            device_id_type=pl.DeviceIdType.MESH,
        )

    def arrived(part, slot):
        message(part, slot, 0, core_other).wait_recv()

    def upward(part, slot, own=False):
        return message(part, slot, 0, me + LANE, own)

    def downward(part, slot, own=False):
        return message(part, slot, 1, me - LANE, own)

    def across(part, slot, own=False):
        return message(part, slot, 2, column_other, own)

    def over(part, slot, own=False):
        return message(part, slot, 3, core_other, own)

    for part in range(2):
        pl.when(place < deep - 1)(lambda: upward(part, me, True).start())
        pl.when(place > 0)(lambda: downward(part, me, True).start())
        across(part, me, True).start()
        over(part, me, True).start()

    def line(distance, part):
        @pl.when(place >= distance)
        def _():
            slot = me - distance * LANE
            arrived(part, slot)
            pl.when(place < deep - 1)(lambda: upward(part, slot).start())
            across(part, slot).start()
            over(part, slot).start()

        @pl.when(place < deep - distance)
        def _():
            slot = me + distance * LANE
            arrived(part, slot)
            pl.when(place > 0)(lambda: downward(part, slot).start())
            across(part, slot).start()
            over(part, slot).start()

    def side(distance, part):
        def relay(slot):
            arrived(part, slot)
            over(part, slot).start()

        if distance == 0:
            relay(column_other)
        else:
            pl.when(place >= distance)(lambda: relay(column_other - distance * LANE))
            pl.when(place < deep - distance)(lambda: relay(column_other + distance * LANE))

    load_q.wait()
    load_kv.wait()
    queries = q_raw.shape[0]
    span_rows = cur_pos_ref.shape[1]
    width = cur_pos_ref.shape[2]
    for r in range(span_rows):
        cosine, sine = turn_tables(
            cur_pos_ref[0, r : r + 1, :], cur_pos_ref[1, r : r + 1, :], cur_pos_ref[2, r : r + 1, :]
        )
        cos_ref[r * width : (r + 1) * width, :] = cosine
        sin_ref[r * width : (r + 1) * width, :] = sine

    def turn_current(first, last):
        for h in range(first, last):
            q_rot[:, head_columns(h)] = turn(q_raw[:, head_columns(h)], cos_ref[...], sin_ref[...])
            k_rot[:, head_columns(h)] = turn(
                kv_raw[0, :, head_columns(h)], cos_ref[...], sin_ref[...]
            )

    turn_current(0, HEADS)
    for distance in range(1, deep):
        for part in range(2):
            line(distance, part)
        for part in range(2):
            side(distance - 1, part)
    for part in range(2):
        side(deep - 1, part)
    for far in range(deep):
        for c in range(COLUMNS):
            for part in range(2):
                arrived(part, far * LANE + c * CORES + 1 - core)
    own_values.wait()

    for e in range(blocks):
        seen = jnp.where(visible_ref[0, e] > 0, 0.0, masked_value)
        bias_ref[e * slots : (e + 1) * slots, :] = jnp.minimum(
            keys[e, :, depth:].astype(jnp.float32), seen
        ).astype(jnp.bfloat16)
    pick = (lax.broadcasted_iota(jnp.int32, (16, HEAD), 1) == 0).astype(jnp.float32)
    bias = lax.dot_general(
        pick.astype(jnp.bfloat16), bias_ref[...], (((1,), (1,)), ((), ())),
        preferred_element_type=jnp.float32,
    )[0:1, :]
    for h in range(HEADS):
        cols = head_columns(h)
        q = q_rot[:, cols]
        near = lax.dot_general(
            q, k_rot[:, cols], (((1,), (1,)), ((), ())), preferred_element_type=jnp.float32
        ) * scale
        far = lax.dot_general(
            q, keys[:, :, cols].reshape(blocks * slots, HEAD), (((1,), (1,)), ((), ())),
            preferred_element_type=jnp.float32,
        ) * scale + bias
        highest = jnp.maximum(
            jnp.max(near, axis=-1, keepdims=True), jnp.max(far, axis=-1, keepdims=True)
        )
        near = jnp.exp(near - highest)
        far = jnp.exp(far - highest)
        total = jnp.sum(near, axis=-1, keepdims=True) + jnp.sum(far, axis=-1, keepdims=True)
        summed = jnp.dot(
            near.astype(jnp.bfloat16), kv_raw[1, :, cols], preferred_element_type=jnp.float32
        ) + jnp.dot(
            far.astype(jnp.bfloat16), values[:, :, cols].reshape(blocks * slots, HEAD),
            preferred_element_type=jnp.float32,
        )
        out_ref[:, cols] = (summed / total).astype(jnp.bfloat16)

    def sent(slot, own=False):
        for part in range(2):
            across(part, slot, own).wait_send()
            over(part, slot, own).wait_send()

    for part in range(2):
        pl.when(place < deep - 1)(lambda: upward(part, me, True).wait_send())
        pl.when(place > 0)(lambda: downward(part, me, True).wait_send())
    sent(me, True)
    for part in range(2):
        over(part, column_other).wait_send()
    for distance in range(1, deep):
        @pl.when(place >= distance)
        def _():
            slot = me - distance * LANE
            sent(slot)
            for part in range(2):
                pl.when(place < deep - 1)(lambda: upward(part, slot).wait_send())
                over(part, column_other - distance * LANE).wait_send()

        @pl.when(place < deep - distance)
        def _():
            slot = me + distance * LANE
            sent(slot)
            for part in range(2):
                pl.when(place > 0)(lambda: downward(part, slot).wait_send())
                over(part, column_other + distance * LANE).wait_send()


def whole_rows(query, cur_kv, cur_pos, cache_kv, cache_pos, counts, visible):
    frames, tile_rows, columns, depth = query.shape
    queries = tile_rows * columns
    slots = cache_kv.shape[2]
    deep = lax.axis_size("tm") // LANE
    blocks = deep * LANE
    vmem = pl.BlockSpec(memory_space=pltpu.VMEM)
    smem = pl.BlockSpec(memory_space=pltpu.SMEM)
    hbm = pl.BlockSpec(memory_space=pl.ANY)
    output = pl.pallas_call(
        lambda *refs: span_kernel(deep, *refs),
        out_shape=jax.ShapeDtypeStruct((queries, depth), jnp.bfloat16),
        in_specs=[hbm, hbm, vmem, vmem, vmem, smem, smem],
        out_specs=vmem,
        scratch_shapes=[
            pltpu.VMEM((queries, depth), jnp.bfloat16),
            pltpu.VMEM((2, queries, depth), jnp.bfloat16),
            pltpu.VMEM((queries, depth), jnp.bfloat16),
            pltpu.VMEM((queries, depth), jnp.bfloat16),
            pltpu.VMEM((queries, HEAD), jnp.float32),
            pltpu.VMEM((queries, HEAD), jnp.float32),
            pltpu.VMEM((blocks, slots, depth + HEAD), jnp.bfloat16),
            pltpu.VMEM((blocks, slots, depth), jnp.bfloat16),
            pltpu.VMEM((blocks * slots, HEAD), jnp.bfloat16),
            pltpu.SemaphoreType.DMA((2,)),
            pltpu.SemaphoreType.DMA,
            pltpu.SemaphoreType.DMA((2, blocks, DIRECTIONS)),
            pltpu.SemaphoreType.DMA((2, blocks)),
        ],
        compiler_params=pltpu.CompilerParams(collective_id=0, has_side_effects=True),
    )(
        query.reshape(queries, depth),
        cur_kv.reshape(2, queries, depth),
        cur_pos.reshape(3, tile_rows, columns),
        cache_kv.reshape(2, slots, depth),
        cache_pos.reshape(3, slots),
        counts,
        visible,
    )
    return output.reshape(frames, tile_rows, columns, depth)


def span_attention(query, *rest):
    fits = (
        lax.axis_size("height") == 1
        and query.shape[0] == 1
        and query.shape[1] <= REACH + 1
        and lax.axis_size("tm") % LANE == 0
    )
    return (whole_rows if fits else per_device)(query, *rest)


def solution(mesh):
    in_specs = (
        P(("group", "tm"), "height", None, None),
        P(None, ("group", "tm"), "height", None, None),
        P(None, ("group", "tm"), "height", None),
        P(("group", "tm"), None, "height", None),
        P(("group", "tm"), None, "height"),
        P(("group", "tm"), "height"),
        P(("group", "tm"), None),
    )
    out_specs = P(("group", "tm"), "height", None, None)
    return jax.shard_map(
        span_attention, mesh=mesh, in_specs=in_specs, out_specs=out_specs, check_vma=False
    )
```

```python
import jax
import jax.numpy as jnp
from jax import lax
from jax.experimental import pallas as pl
from jax.experimental.pallas import tpu as pltpu
from jax.sharding import PartitionSpec as P

HEADS = 12
HEAD = 128
REACH = 2


masked_value = -1e30


def extended(cells, sides, width):
    for axis, dim in sides:
        count = lax.axis_size(axis)
        ends = count - 1
        head = lax.slice_in_dim(cells, 0, width, axis=dim)
        tail = lax.slice_in_dim(cells, cells.shape[dim] - width, cells.shape[dim], axis=dim)
        cells = jnp.concatenate(
            [
                lax.ppermute(tail, axis, [(i, (i + 1) % count) for i in range(ends)]),
                cells,
                lax.ppermute(head, axis, [((i + 1) % count, i) for i in range(ends)]),
            ],
            axis=dim,
        )
    return cells


def rope_tables():
    half = HEAD // 2
    index = jnp.arange(half)
    first = HEAD // 8
    second = 3 * HEAD // 16
    member = (index >= first).astype(jnp.int32) + (index >= first + second).astype(jnp.int32)
    begin = jnp.where(member == 0, 0, jnp.where(member == 1, first, first + second))
    length = jnp.where(member == 0, first, jnp.where(member == 1, second, half - first - second))
    frequency = jnp.power(
        10000.0, -(index - begin).astype(jnp.float32) / length.astype(jnp.float32)
    )
    select = (member[None, :] == jnp.arange(3)[:, None]).astype(jnp.float32) * frequency[None, :]
    return select


def rotate(vectors, pos_time, pos_row, pos_column):
    select = rope_tables()
    angle = (
        pos_time.astype(jnp.float32)[..., None] * select[0]
        + pos_row.astype(jnp.float32)[..., None] * select[1]
        + pos_column.astype(jnp.float32)[..., None] * select[2]
    )
    cosine = jnp.cos(angle)[..., None, :]
    sine = jnp.sin(angle)[..., None, :]
    shaped = vectors.astype(jnp.float32).reshape(vectors.shape[:-1] + (HEADS, 2, HEAD // 2))
    lower = shaped[..., 0, :]
    upper = shaped[..., 1, :]
    turned = jnp.stack([lower * cosine - upper * sine, upper * cosine + lower * sine], axis=-2)
    return turned.reshape(vectors.shape).astype(jnp.bfloat16)


def per_device(query, cur_kv, cur_pos, cache_kv, cache_pos, counts, visible):
    frames, tile_rows, columns, depth = query.shape
    queries = tile_rows * columns
    scale = HEAD ** (-0.5)
    tile_index = lax.axis_index("height")
    frame_rows = tile_rows * lax.axis_size("height")
    q_rot = rotate(query, cur_pos[0], cur_pos[1], cur_pos[2]).reshape(frames, queries, HEADS, HEAD)
    q_heads = jnp.transpose(q_rot, (0, 2, 1, 3))
    k_rot = rotate(cur_kv[0], cur_pos[0], cur_pos[1], cur_pos[2])
    local_pair = jnp.stack([k_rot, cur_kv[1]])
    padded = extended(local_pair, (("height", 2),), REACH)
    extent = tile_rows + 2 * REACH
    local_keys = jnp.transpose(
        padded[0].reshape(frames, extent * columns, HEADS, HEAD), (0, 2, 1, 3)
    )
    local_values = jnp.transpose(
        padded[1].reshape(frames, extent * columns, HEADS, HEAD), (0, 2, 1, 3)
    )
    query_row = tile_index * tile_rows + jnp.arange(queries) // columns
    key_row = tile_index * tile_rows - REACH + jnp.arange(extent * columns) // columns
    local_ok = (
        (key_row[None, :] >= 0)
        & (key_row[None, :] < frame_rows)
        & (jnp.abs(query_row[:, None] - key_row[None, :]) <= REACH)
    )
    local_bias = jnp.where(local_ok, 0.0, masked_value).astype(jnp.float32)
    scores = (
        jnp.einsum("fhqd,fhkd->fhqk", q_heads, local_keys, preferred_element_type=jnp.float32)
        * scale
        + local_bias[None, None]
    )
    highest = jnp.max(scores, axis=-1)
    weights = jnp.exp(scores - highest[..., None])
    totals = jnp.sum(weights, axis=-1)
    summed = jnp.einsum(
        "fhqk,fhkd->fhqd",
        weights.astype(jnp.bfloat16),
        local_values,
        preferred_element_type=jnp.float32,
    )
    slots = cache_kv.shape[2]
    slot_index = jnp.arange(slots)
    pair_piece = lax.all_gather(cache_kv, "tm", axis=0, tiled=True)
    position_piece = lax.all_gather(cache_pos, "tm", axis=0, tiled=True)
    count_piece = lax.all_gather(counts, "tm", axis=0, tiled=True)
    turned = rotate(
        pair_piece[:, 0], position_piece[:, 0], position_piece[:, 1], position_piece[:, 2]
    )
    blocks = turned.shape[0]
    live = count_piece[:, 0]
    usable = (
        (visible[:, :, None] > 0) & (slot_index[None, None, :] < live[None, :, None])
    ).reshape(frames, blocks * slots)
    block_bias = jnp.where(usable, 0.0, masked_value).astype(jnp.float32)
    flat_keys = jnp.transpose(turned.reshape(blocks * slots, HEADS, HEAD), (1, 0, 2))
    flat_values = jnp.transpose(pair_piece[:, 1].reshape(blocks * slots, HEADS, HEAD), (1, 0, 2))
    block_scores = (
        jnp.einsum("fhqd,hkd->fhqk", q_heads, flat_keys, preferred_element_type=jnp.float32) * scale
        + block_bias[:, None, None, :]
    )
    new_max = jnp.maximum(highest, jnp.max(block_scores, axis=-1))
    block_weights = jnp.exp(block_scores - new_max[..., None])
    fading = jnp.exp(highest - new_max)
    added = jnp.einsum(
        "fhqk,hkd->fhqd",
        block_weights.astype(jnp.bfloat16),
        flat_values,
        preferred_element_type=jnp.float32,
    )
    final_total = totals * fading + jnp.sum(block_weights, axis=-1)
    final_sum = summed * fading[..., None] + added
    output = (final_sum / final_total[..., None]).astype(jnp.bfloat16)
    output = jnp.transpose(output, (0, 2, 1, 3))
    return output.reshape(frames, tile_rows, columns, depth)


CORES = 2
COLUMNS = 2
LANE = CORES * COLUMNS
DIRECTIONS = 4


def frequency_rows(axis, shape):
    half = HEAD // 2
    index = lax.broadcasted_iota(jnp.int32, shape, axis) % half
    first = HEAD // 8
    second = 3 * HEAD // 16
    member = (index >= first).astype(jnp.int32) + (index >= first + second).astype(jnp.int32)
    begin = jnp.where(member == 0, 0, jnp.where(member == 1, first, first + second))
    length = jnp.where(member == 0, first, jnp.where(member == 1, second, half - first - second))
    ratio = (index - begin).astype(jnp.float32) / length.astype(jnp.float32)
    return member, jnp.exp(-ratio * 9.210340371976184)


def turn_tables(pos_time, pos_row, pos_column):
    tokens = pos_time.shape[-1]
    member, _ = frequency_rows(0, (HEAD, tokens))
    chosen = jnp.where(member == 0, pos_time, jnp.where(member == 1, pos_row, pos_column))
    eye = (
        lax.broadcasted_iota(jnp.int32, (tokens, tokens), 0)
        == lax.broadcasted_iota(jnp.int32, (tokens, tokens), 1)
    ).astype(jnp.float32).astype(jnp.bfloat16)
    spread = lax.dot_general(
        eye,
        chosen.astype(jnp.float32).astype(jnp.bfloat16),
        (((1,), (1,)), ((), ())),
        preferred_element_type=jnp.float32,
    )
    _, frequency = frequency_rows(1, (1, HEAD))
    angle = spread * frequency
    lane = lax.broadcasted_iota(jnp.int32, (tokens, HEAD), 1)
    sine = jnp.sin(angle)
    return jnp.cos(angle), jnp.where(lane < HEAD // 2, -sine, sine)


def turn(vectors, cosine, sine):
    wide = vectors.astype(jnp.float32)
    return (wide * cosine + pltpu.roll(wide, HEAD // 2, 1) * sine).astype(jnp.bfloat16)


def fold(weights):
    pieces = [weights[:, i : i + HEAD] for i in range(0, weights.shape[1], HEAD)]
    return sum(pieces[1:], pieces[0])


def head_columns(h):
    return slice(h * HEAD, (h + 1) * HEAD)


def span_kernel(
    deep, q_hbm, kv_hbm, cur_pos_ref, cache_ref, cache_pos_hbm, count_ref, visible_ref, out_ref,
    q_raw, kv_raw, q_rot, k_rot, cos_ref, sin_ref, keys, values, kept_pos, top_ref, total_ref, sum_ref, load_sem, own_sem,
    send_sem, recv_sem,
):
    me = lax.axis_index("tm")
    place = me // LANE
    column = (me % LANE) // CORES
    core = me % CORES
    slots = cache_ref.shape[1]
    depth = cache_ref.shape[2]
    blocks = deep * LANE
    scale = HEAD ** (-0.5)
    core_other = me + 1 - 2 * core
    column_other = me + CORES - 2 * CORES * column
    barrier = pltpu.get_barrier_semaphore()

    def greet(device):
        pl.semaphore_signal(
            barrier, inc=1, device_id={"tm": device}, device_id_type=pl.DeviceIdType.MESH
        )

    load_pos = pltpu.make_async_copy(cache_pos_hbm, kept_pos, load_sem.at[2])
    load_pos.start()
    greet(core_other)
    greet(column_other)
    pl.when(place > 0)(lambda: greet(me - LANE))
    pl.when(place < deep - 1)(lambda: greet(me + LANE))

    load_q = pltpu.make_async_copy(q_hbm, q_raw, load_sem.at[0])
    load_kv = pltpu.make_async_copy(kv_hbm, kv_raw, load_sem.at[1])
    own_values = pltpu.make_async_copy(cache_ref.at[1], values.at[me], own_sem)
    load_q.start()
    load_kv.start()
    own_values.start()

    load_pos.wait()
    cosine, sine = turn_tables(kept_pos[0], kept_pos[1], kept_pos[2])
    for h in range(HEADS):
        keys[me, :, head_columns(h)] = turn(cache_ref[0, :, head_columns(h)], cosine, sine)
    row = lax.broadcasted_iota(jnp.int32, (slots, HEAD), 0)
    keys[me, :, depth:] = jnp.where(row < count_ref[0, 0], 0.0, masked_value).astype(jnp.bfloat16)

    pl.semaphore_wait(
        barrier,
        2 + (place > 0).astype(jnp.int32) + (place < deep - 1).astype(jnp.int32),
    )

    def message(part, slot, direction, device, own=False):
        buffer = (values, keys)[part]
        source = cache_ref.at[1] if own and part == 0 else buffer.at[slot]
        return pltpu.make_async_remote_copy(
            src_ref=source,
            dst_ref=buffer.at[slot],
            send_sem=send_sem.at[part, slot, direction],
            recv_sem=recv_sem.at[part, slot],
            device_id={"tm": device},
            device_id_type=pl.DeviceIdType.MESH,
        )

    def arrived(part, slot):
        message(part, slot, 0, core_other).wait_recv()

    def upward(part, slot, own=False):
        return message(part, slot, 0, me + LANE, own)

    def downward(part, slot, own=False):
        return message(part, slot, 1, me - LANE, own)

    def across(part, slot, own=False):
        return message(part, slot, 2, column_other, own)

    def over(part, slot, own=False):
        return message(part, slot, 3, core_other, own)

    for part in range(2):
        pl.when(place < deep - 1)(lambda: upward(part, me, True).start())
        pl.when(place > 0)(lambda: downward(part, me, True).start())
        across(part, me, True).start()
        over(part, me, True).start()

    def line(distance, part):
        @pl.when(place >= distance)
        def _():
            slot = me - distance * LANE
            arrived(part, slot)
            pl.when(place < deep - 1)(lambda: upward(part, slot).start())
            across(part, slot).start()
            over(part, slot).start()

        @pl.when(place < deep - distance)
        def _():
            slot = me + distance * LANE
            arrived(part, slot)
            pl.when(place > 0)(lambda: downward(part, slot).start())
            across(part, slot).start()
            over(part, slot).start()

    def side(distance, part):
        def relay(slot):
            arrived(part, slot)
            over(part, slot).start()

        if distance == 0:
            relay(column_other)
        else:
            pl.when(place >= distance)(lambda: relay(column_other - distance * LANE))
            pl.when(place < deep - distance)(lambda: relay(column_other + distance * LANE))

    load_q.wait()
    load_kv.wait()
    queries = q_raw.shape[0]
    span_rows = cur_pos_ref.shape[1]
    width = cur_pos_ref.shape[2]
    for r in range(span_rows):
        cosine, sine = turn_tables(
            cur_pos_ref[0, r : r + 1, :], cur_pos_ref[1, r : r + 1, :], cur_pos_ref[2, r : r + 1, :]
        )
        cos_ref[r * width : (r + 1) * width, :] = cosine
        sin_ref[r * width : (r + 1) * width, :] = sine

    def turn_current(first, last):
        for h in range(first, last):
            q_rot[:, head_columns(h)] = turn(q_raw[:, head_columns(h)], cos_ref[...], sin_ref[...])
            k_rot[:, head_columns(h)] = turn(
                kv_raw[0, :, head_columns(h)], cos_ref[...], sin_ref[...]
            )

    turn_current(0, HEADS)
    pick = (lax.broadcasted_iota(jnp.int32, (16, HEAD), 1) == 0).astype(jnp.float32)
    pick = pick.astype(jnp.bfloat16)
    transposed = (((1,), (1,)), ((), ()))
    for h in range(HEADS):
        cols = head_columns(h)
        scores = lax.dot_general(
            q_rot[:, cols], k_rot[:, cols], transposed, preferred_element_type=jnp.float32
        ) * scale
        highest = jnp.max(scores, axis=-1, keepdims=True)
        weights = jnp.exp(scores - highest)
        top_ref[:, cols] = jnp.broadcast_to(highest, (queries, HEAD))
        total_ref[:, cols] = fold(weights)
        sum_ref[:, cols] = jnp.dot(
            weights.astype(jnp.bfloat16), kv_raw[1, :, cols], preferred_element_type=jnp.float32
        )

    def plane(number, last):
        first = number * LANE
        for c in range(COLUMNS):
            for part in range(2):
                arrived(part, first + c * CORES + 1 - core)
        spans = []
        for i in range(LANE):
            seen = jnp.where(visible_ref[0, first + i] > 0, 0.0, masked_value)
            spans.append(
                jnp.minimum(keys[first + i, :, depth:].astype(jnp.float32), seen)
            )
        bias = lax.dot_general(
            pick, jnp.concatenate(spans, axis=0).astype(jnp.bfloat16), transposed,
            preferred_element_type=jnp.float32,
        )[0:1, :]
        for h in range(HEADS):
            cols = head_columns(h)
            block = keys[pl.ds(first, LANE), :, cols].reshape(LANE * slots, HEAD)
            scores = lax.dot_general(
                q_rot[:, cols], block, transposed, preferred_element_type=jnp.float32
            ) * scale + bias
            old = top_ref[:, cols]
            highest = jnp.maximum(old, jnp.max(scores, axis=-1, keepdims=True))
            fading = jnp.exp(old - highest)
            weights = jnp.exp(scores - highest[:, 0:1])
            total = total_ref[:, cols] * fading + fold(weights)
            summed = sum_ref[:, cols] * fading + jnp.dot(
                weights.astype(jnp.bfloat16),
                values[pl.ds(first, LANE), :, cols].reshape(LANE * slots, HEAD),
                preferred_element_type=jnp.float32,
            )
            if last:
                out_ref[:, cols] = (
                    summed / jnp.sum(total, axis=-1, keepdims=True)
                ).astype(jnp.bfloat16)
            else:
                top_ref[:, cols] = highest
                total_ref[:, cols] = total
                sum_ref[:, cols] = summed

    nearest = [sorted(range(deep), key=lambda other: abs(other - z)) for z in range(deep)]

    def ordered(k):
        number = 0
        for z in range(deep):
            number = number + (place == z).astype(jnp.int32) * nearest[z][k]
        return number

    own_values.wait()
    for distance in range(1, deep):
        for part in range(2):
            line(distance, part)
        for part in range(2):
            side(distance - 1, part)
        plane(ordered(distance - 1), False)
    for part in range(2):
        side(deep - 1, part)
    plane(ordered(deep - 1), True)

    def sent(slot, own=False):
        for part in range(2):
            across(part, slot, own).wait_send()
            over(part, slot, own).wait_send()

    for part in range(2):
        pl.when(place < deep - 1)(lambda: upward(part, me, True).wait_send())
        pl.when(place > 0)(lambda: downward(part, me, True).wait_send())
    sent(me, True)
    for part in range(2):
        over(part, column_other).wait_send()
    for distance in range(1, deep):
        @pl.when(place >= distance)
        def _():
            slot = me - distance * LANE
            sent(slot)
            for part in range(2):
                pl.when(place < deep - 1)(lambda: upward(part, slot).wait_send())
                over(part, column_other - distance * LANE).wait_send()

        @pl.when(place < deep - distance)
        def _():
            slot = me + distance * LANE
            sent(slot)
            for part in range(2):
                pl.when(place > 0)(lambda: downward(part, slot).wait_send())
                over(part, column_other + distance * LANE).wait_send()


def whole_rows(query, cur_kv, cur_pos, cache_kv, cache_pos, counts, visible):
    frames, tile_rows, columns, depth = query.shape
    queries = tile_rows * columns
    slots = cache_kv.shape[2]
    deep = lax.axis_size("tm") // LANE
    blocks = deep * LANE
    vmem = pl.BlockSpec(memory_space=pltpu.VMEM)
    smem = pl.BlockSpec(memory_space=pltpu.SMEM)
    hbm = pl.BlockSpec(memory_space=pltpu.HBM)
    output = pl.pallas_call(
        lambda *refs: span_kernel(deep, *refs),
        out_shape=jax.ShapeDtypeStruct((queries, depth), jnp.bfloat16),
        in_specs=[hbm, hbm, vmem, vmem, hbm, smem, smem],
        out_specs=vmem,
        scratch_shapes=[
            pltpu.VMEM((queries, depth), jnp.bfloat16),
            pltpu.VMEM((2, queries, depth), jnp.bfloat16),
            pltpu.VMEM((queries, depth), jnp.bfloat16),
            pltpu.VMEM((queries, depth), jnp.bfloat16),
            pltpu.VMEM((queries, HEAD), jnp.float32),
            pltpu.VMEM((queries, HEAD), jnp.float32),
            pltpu.VMEM((blocks, slots, depth + HEAD), jnp.bfloat16),
            pltpu.VMEM((blocks, slots, depth), jnp.bfloat16),
            pltpu.VMEM((3, 1, slots), jnp.int32),
            pltpu.VMEM((queries, depth), jnp.float32),
            pltpu.VMEM((queries, depth), jnp.float32),
            pltpu.VMEM((queries, depth), jnp.float32),
            pltpu.SemaphoreType.DMA((3,)),
            pltpu.SemaphoreType.DMA,
            pltpu.SemaphoreType.DMA((2, blocks, DIRECTIONS)),
            pltpu.SemaphoreType.DMA((2, blocks)),
        ],
        compiler_params=pltpu.CompilerParams(
            collective_id=0, has_side_effects=True, vmem_limit_bytes=24 * 1024 * 1024
        ),
    )(
        query.reshape(queries, depth),
        cur_kv.reshape(2, queries, depth),
        cur_pos.reshape(3, tile_rows, columns),
        cache_kv.reshape(2, slots, depth),
        jnp.transpose(cache_pos, (1, 0, 2)),
        counts,
        visible,
    )
    return output.reshape(frames, tile_rows, columns, depth)


def span_attention(query, *rest):
    fits = (
        lax.axis_size("height") == 1
        and query.shape[0] == 1
        and query.shape[1] <= REACH + 1
        and query.shape[1] * query.shape[2] % HEAD == 0
        and lax.axis_size("tm") % LANE == 0
    )
    return (whole_rows if fits else per_device)(query, *rest)


def solution(mesh):
    in_specs = (
        P(("group", "tm"), "height", None, None),
        P(None, ("group", "tm"), "height", None, None),
        P(None, ("group", "tm"), "height", None),
        P(("group", "tm"), None, "height", None),
        P(("group", "tm"), None, "height"),
        P(("group", "tm"), "height"),
        P(("group", "tm"), None),
    )
    out_specs = P(("group", "tm"), "height", None, None)
    return jax.shard_map(
        span_attention, mesh=mesh, in_specs=in_specs, out_specs=out_specs, check_vma=False
    )
```

```python
import jax
import jax.numpy as jnp
from jax import lax
from jax.experimental import pallas as pl
from jax.experimental.pallas import tpu as pltpu
from jax.sharding import PartitionSpec as P

HEADS = 12
HEAD = 128
REACH = 2


masked_value = -1e30


def extended(cells, sides, width):
    for axis, dim in sides:
        count = lax.axis_size(axis)
        ends = count - 1
        head = lax.slice_in_dim(cells, 0, width, axis=dim)
        tail = lax.slice_in_dim(cells, cells.shape[dim] - width, cells.shape[dim], axis=dim)
        cells = jnp.concatenate(
            [
                lax.ppermute(tail, axis, [(i, (i + 1) % count) for i in range(ends)]),
                cells,
                lax.ppermute(head, axis, [((i + 1) % count, i) for i in range(ends)]),
            ],
            axis=dim,
        )
    return cells


def rope_tables():
    half = HEAD // 2
    index = jnp.arange(half)
    first = HEAD // 8
    second = 3 * HEAD // 16
    member = (index >= first).astype(jnp.int32) + (index >= first + second).astype(jnp.int32)
    begin = jnp.where(member == 0, 0, jnp.where(member == 1, first, first + second))
    length = jnp.where(member == 0, first, jnp.where(member == 1, second, half - first - second))
    frequency = jnp.power(
        10000.0, -(index - begin).astype(jnp.float32) / length.astype(jnp.float32)
    )
    select = (member[None, :] == jnp.arange(3)[:, None]).astype(jnp.float32) * frequency[None, :]
    return select


def rotate(vectors, pos_time, pos_row, pos_column):
    select = rope_tables()
    angle = (
        pos_time.astype(jnp.float32)[..., None] * select[0]
        + pos_row.astype(jnp.float32)[..., None] * select[1]
        + pos_column.astype(jnp.float32)[..., None] * select[2]
    )
    cosine = jnp.cos(angle)[..., None, :]
    sine = jnp.sin(angle)[..., None, :]
    shaped = vectors.astype(jnp.float32).reshape(vectors.shape[:-1] + (HEADS, 2, HEAD // 2))
    lower = shaped[..., 0, :]
    upper = shaped[..., 1, :]
    turned = jnp.stack([lower * cosine - upper * sine, upper * cosine + lower * sine], axis=-2)
    return turned.reshape(vectors.shape).astype(jnp.bfloat16)


def per_device(query, cur_kv, cur_pos, cache_kv, cache_pos, counts, visible):
    frames, tile_rows, columns, depth = query.shape
    queries = tile_rows * columns
    scale = HEAD ** (-0.5)
    tile_index = lax.axis_index("height")
    frame_rows = tile_rows * lax.axis_size("height")
    q_rot = rotate(query, cur_pos[0], cur_pos[1], cur_pos[2]).reshape(frames, queries, HEADS, HEAD)
    q_heads = jnp.transpose(q_rot, (0, 2, 1, 3))
    k_rot = rotate(cur_kv[0], cur_pos[0], cur_pos[1], cur_pos[2])
    local_pair = jnp.stack([k_rot, cur_kv[1]])
    padded = extended(local_pair, (("height", 2),), REACH)
    extent = tile_rows + 2 * REACH
    local_keys = jnp.transpose(
        padded[0].reshape(frames, extent * columns, HEADS, HEAD), (0, 2, 1, 3)
    )
    local_values = jnp.transpose(
        padded[1].reshape(frames, extent * columns, HEADS, HEAD), (0, 2, 1, 3)
    )
    query_row = tile_index * tile_rows + jnp.arange(queries) // columns
    key_row = tile_index * tile_rows - REACH + jnp.arange(extent * columns) // columns
    local_ok = (
        (key_row[None, :] >= 0)
        & (key_row[None, :] < frame_rows)
        & (jnp.abs(query_row[:, None] - key_row[None, :]) <= REACH)
    )
    local_bias = jnp.where(local_ok, 0.0, masked_value).astype(jnp.float32)
    scores = (
        jnp.einsum("fhqd,fhkd->fhqk", q_heads, local_keys, preferred_element_type=jnp.float32)
        * scale
        + local_bias[None, None]
    )
    highest = jnp.max(scores, axis=-1)
    weights = jnp.exp(scores - highest[..., None])
    totals = jnp.sum(weights, axis=-1)
    summed = jnp.einsum(
        "fhqk,fhkd->fhqd",
        weights.astype(jnp.bfloat16),
        local_values,
        preferred_element_type=jnp.float32,
    )
    slots = cache_kv.shape[2]
    slot_index = jnp.arange(slots)
    pair_piece = lax.all_gather(cache_kv, "tm", axis=0, tiled=True)
    position_piece = lax.all_gather(cache_pos, "tm", axis=0, tiled=True)
    count_piece = lax.all_gather(counts, "tm", axis=0, tiled=True)
    turned = rotate(
        pair_piece[:, 0], position_piece[:, 0], position_piece[:, 1], position_piece[:, 2]
    )
    blocks = turned.shape[0]
    live = count_piece[:, 0]
    usable = (
        (visible[:, :, None] > 0) & (slot_index[None, None, :] < live[None, :, None])
    ).reshape(frames, blocks * slots)
    block_bias = jnp.where(usable, 0.0, masked_value).astype(jnp.float32)
    flat_keys = jnp.transpose(turned.reshape(blocks * slots, HEADS, HEAD), (1, 0, 2))
    flat_values = jnp.transpose(pair_piece[:, 1].reshape(blocks * slots, HEADS, HEAD), (1, 0, 2))
    block_scores = (
        jnp.einsum("fhqd,hkd->fhqk", q_heads, flat_keys, preferred_element_type=jnp.float32) * scale
        + block_bias[:, None, None, :]
    )
    new_max = jnp.maximum(highest, jnp.max(block_scores, axis=-1))
    block_weights = jnp.exp(block_scores - new_max[..., None])
    fading = jnp.exp(highest - new_max)
    added = jnp.einsum(
        "fhqk,hkd->fhqd",
        block_weights.astype(jnp.bfloat16),
        flat_values,
        preferred_element_type=jnp.float32,
    )
    final_total = totals * fading + jnp.sum(block_weights, axis=-1)
    final_sum = summed * fading[..., None] + added
    output = (final_sum / final_total[..., None]).astype(jnp.bfloat16)
    output = jnp.transpose(output, (0, 2, 1, 3))
    return output.reshape(frames, tile_rows, columns, depth)


CORES = 2
COLUMNS = 2
LANE = CORES * COLUMNS
DIRECTIONS = 4


def frequency_rows(axis, shape):
    half = HEAD // 2
    index = lax.broadcasted_iota(jnp.int32, shape, axis) % half
    first = HEAD // 8
    second = 3 * HEAD // 16
    member = (index >= first).astype(jnp.int32) + (index >= first + second).astype(jnp.int32)
    begin = jnp.where(member == 0, 0, jnp.where(member == 1, first, first + second))
    length = jnp.where(member == 0, first, jnp.where(member == 1, second, half - first - second))
    ratio = (index - begin).astype(jnp.float32) / length.astype(jnp.float32)
    return member, jnp.exp(-ratio * 9.210340371976184)


def turn_tables(pos_time, pos_row, pos_column):
    tokens = pos_time.shape[-1]
    member, _ = frequency_rows(0, (HEAD, tokens))
    chosen = jnp.where(member == 0, pos_time, jnp.where(member == 1, pos_row, pos_column))
    eye = (
        lax.broadcasted_iota(jnp.int32, (tokens, tokens), 0)
        == lax.broadcasted_iota(jnp.int32, (tokens, tokens), 1)
    ).astype(jnp.float32).astype(jnp.bfloat16)
    spread = lax.dot_general(
        eye,
        chosen.astype(jnp.float32).astype(jnp.bfloat16),
        (((1,), (1,)), ((), ())),
        preferred_element_type=jnp.float32,
    )
    _, frequency = frequency_rows(1, (1, HEAD))
    angle = spread * frequency
    lane = lax.broadcasted_iota(jnp.int32, (tokens, HEAD), 1)
    sine = jnp.sin(angle)
    return jnp.cos(angle), jnp.where(lane < HEAD // 2, -sine, sine)


def turn(vectors, cosine, sine):
    wide = vectors.astype(jnp.float32)
    return (wide * cosine + pltpu.roll(wide, HEAD // 2, 1) * sine).astype(jnp.bfloat16)


def fold(weights):
    pieces = [weights[:, i : i + HEAD] for i in range(0, weights.shape[1], HEAD)]
    return sum(pieces[1:], pieces[0])


def head_columns(h):
    return slice(h * HEAD, (h + 1) * HEAD)


def span_kernel(
    deep, q_hbm, kv_hbm, cur_pos_ref, cache_ref, cache_pos_hbm, count_ref, visible_ref, out_ref,
    q_raw, kv_raw, q_rot, k_rot, cos_ref, sin_ref, keys, values, kept_pos, top_ref, total_ref, sum_ref, bias_ref, load_sem, own_sem,
    send_sem, recv_sem,
):
    me = lax.axis_index("tm")
    place = me // LANE
    column = (me % LANE) // CORES
    core = me % CORES
    slots = cache_ref.shape[1]
    depth = cache_ref.shape[2]
    blocks = deep * LANE
    scale = HEAD ** (-0.5)
    core_other = me + 1 - 2 * core
    column_other = me + CORES - 2 * CORES * column
    barrier = pltpu.get_barrier_semaphore()

    def greet(device):
        pl.semaphore_signal(
            barrier, inc=1, device_id={"tm": device}, device_id_type=pl.DeviceIdType.MESH
        )

    load_pos = pltpu.make_async_copy(cache_pos_hbm, kept_pos, load_sem.at[2])
    load_pos.start()
    greet(core_other)
    greet(column_other)
    pl.when(place > 0)(lambda: greet(me - LANE))
    pl.when(place < deep - 1)(lambda: greet(me + LANE))

    load_q = pltpu.make_async_copy(q_hbm, q_raw, load_sem.at[0])
    load_kv = pltpu.make_async_copy(kv_hbm, kv_raw, load_sem.at[1])
    own_values = pltpu.make_async_copy(cache_ref.at[1], values.at[me], own_sem)
    load_q.start()
    load_kv.start()
    own_values.start()

    load_pos.wait()
    cosine, sine = turn_tables(kept_pos[0], kept_pos[1], kept_pos[2])
    for h in range(HEADS):
        keys[me, :, head_columns(h)] = turn(cache_ref[0, :, head_columns(h)], cosine, sine)
    row = lax.broadcasted_iota(jnp.int32, (slots, HEAD), 0)
    keys[me, :, depth:] = jnp.where(row < count_ref[0, 0], 0.0, masked_value).astype(jnp.bfloat16)

    pl.semaphore_wait(
        barrier,
        2 + (place > 0).astype(jnp.int32) + (place < deep - 1).astype(jnp.int32),
    )

    def message(part, slot, direction, device, own=False):
        buffer = (values, keys)[part]
        source = cache_ref.at[1] if own and part == 0 else buffer.at[slot]
        return pltpu.make_async_remote_copy(
            src_ref=source,
            dst_ref=buffer.at[slot],
            send_sem=send_sem.at[part, slot, direction],
            recv_sem=recv_sem.at[part, slot],
            device_id={"tm": device},
            device_id_type=pl.DeviceIdType.MESH,
        )

    def arrived(part, slot):
        message(part, slot, 0, core_other).wait_recv()

    def upward(part, slot, own=False):
        return message(part, slot, 0, me + LANE, own)

    def downward(part, slot, own=False):
        return message(part, slot, 1, me - LANE, own)

    def across(part, slot, own=False):
        return message(part, slot, 2, column_other, own)

    def over(part, slot, own=False):
        return message(part, slot, 3, core_other, own)

    for part in range(2):
        pl.when(place < deep - 1)(lambda: upward(part, me, True).start())
        pl.when(place > 0)(lambda: downward(part, me, True).start())
        across(part, me, True).start()
        over(part, me, True).start()

    def line(distance, part):
        @pl.when(place >= distance)
        def _():
            slot = me - distance * LANE
            arrived(part, slot)
            pl.when(place < deep - 1)(lambda: upward(part, slot).start())
            across(part, slot).start()
            over(part, slot).start()

        @pl.when(place < deep - distance)
        def _():
            slot = me + distance * LANE
            arrived(part, slot)
            pl.when(place > 0)(lambda: downward(part, slot).start())
            across(part, slot).start()
            over(part, slot).start()

    def side(distance, part):
        def relay(slot):
            arrived(part, slot)
            over(part, slot).start()

        if distance == 0:
            relay(column_other)
        else:
            pl.when(place >= distance)(lambda: relay(column_other - distance * LANE))
            pl.when(place < deep - distance)(lambda: relay(column_other + distance * LANE))

    load_q.wait()
    load_kv.wait()
    queries = q_raw.shape[0]
    span_rows = cur_pos_ref.shape[1]
    width = cur_pos_ref.shape[2]
    for r in range(span_rows):
        cosine, sine = turn_tables(
            cur_pos_ref[0, r : r + 1, :], cur_pos_ref[1, r : r + 1, :], cur_pos_ref[2, r : r + 1, :]
        )
        cos_ref[r * width : (r + 1) * width, :] = cosine
        sin_ref[r * width : (r + 1) * width, :] = sine

    def turn_current(first, last):
        for h in range(first, last):
            q_rot[:, head_columns(h)] = turn(q_raw[:, head_columns(h)], cos_ref[...], sin_ref[...])
            k_rot[:, head_columns(h)] = turn(
                kv_raw[0, :, head_columns(h)], cos_ref[...], sin_ref[...]
            )

    turn_current(0, HEADS)
    pick = (lax.broadcasted_iota(jnp.int32, (16, HEAD), 1) == 0).astype(jnp.float32)
    pick = pick.astype(jnp.bfloat16)
    transposed = (((1,), (1,)), ((), ()))
    def near_attention():
        for h in range(HEADS):
            cols = head_columns(h)
            scores = lax.dot_general(
                q_rot[:, cols], k_rot[:, cols], transposed, preferred_element_type=jnp.float32
            ) * scale
            highest = jnp.max(scores, axis=-1, keepdims=True)
            weights = jnp.exp(scores - highest)
            top_ref[:, cols] = jnp.broadcast_to(highest, (queries, HEAD))
            total_ref[:, cols] = fold(weights)
            sum_ref[:, cols] = jnp.dot(
                weights.astype(jnp.bfloat16), kv_raw[1, :, cols], preferred_element_type=jnp.float32
            )

    def gather(number):
        first = number * LANE
        for c in range(COLUMNS):
            for part in range(2):
                arrived(part, first + c * CORES + 1 - core)
        spans = []
        for i in range(LANE):
            seen = jnp.where(visible_ref[0, first + i] > 0, 0.0, masked_value)
            spans.append(
                jnp.minimum(keys[first + i, :, depth:].astype(jnp.float32), seen)
            )
        bias_ref[...] = lax.dot_general(
            pick, jnp.concatenate(spans, axis=0).astype(jnp.bfloat16), transposed,
            preferred_element_type=jnp.float32,
        )

    def plane(number, start, stop, last):
        first = number * LANE
        bias = bias_ref[0:1, :]
        for h in range(start, stop):
            cols = head_columns(h)
            block = keys[pl.ds(first, LANE), :, cols].reshape(LANE * slots, HEAD)
            scores = lax.dot_general(
                q_rot[:, cols], block, transposed, preferred_element_type=jnp.float32
            ) * scale + bias
            old = top_ref[:, cols]
            highest = jnp.maximum(old, jnp.max(scores, axis=-1, keepdims=True))
            fading = jnp.exp(old - highest)
            weights = jnp.exp(scores - highest[:, 0:1])
            total = total_ref[:, cols] * fading + fold(weights)
            summed = sum_ref[:, cols] * fading + jnp.dot(
                weights.astype(jnp.bfloat16),
                values[pl.ds(first, LANE), :, cols].reshape(LANE * slots, HEAD),
                preferred_element_type=jnp.float32,
            )
            if last:
                out_ref[:, cols] = (
                    summed / jnp.sum(total, axis=-1, keepdims=True)
                ).astype(jnp.bfloat16)
            else:
                top_ref[:, cols] = highest
                total_ref[:, cols] = total
                sum_ref[:, cols] = summed

    nearest = [sorted(range(deep), key=lambda other: abs(other - z)) for z in range(deep)]

    def ordered(k):
        number = 0
        for z in range(deep):
            number = number + (place == z).astype(jnp.int32) * nearest[z][k]
        return number

    own_values.wait()
    half = HEADS // 2
    number = None
    for distance in range(1, deep):
        for part in range(2):
            line(distance, part)
            side(distance - 1, part)
            if distance == 1 and part == 0:
                near_attention()
                continue
            if part == 0:
                plane(number, half, HEADS, False)
            else:
                number = ordered(distance - 1)
                gather(number)
                plane(number, 0, half, False)
    plane(number, half, HEADS, False)
    for part in range(2):
        side(deep - 1, part)
    number = ordered(deep - 1)
    gather(number)
    plane(number, 0, HEADS, True)

    def sent(slot, own=False):
        for part in range(2):
            across(part, slot, own).wait_send()
            over(part, slot, own).wait_send()

    for part in range(2):
        pl.when(place < deep - 1)(lambda: upward(part, me, True).wait_send())
        pl.when(place > 0)(lambda: downward(part, me, True).wait_send())
    sent(me, True)
    for part in range(2):
        over(part, column_other).wait_send()
    for distance in range(1, deep):
        @pl.when(place >= distance)
        def _():
            slot = me - distance * LANE
            sent(slot)
            for part in range(2):
                pl.when(place < deep - 1)(lambda: upward(part, slot).wait_send())
                over(part, column_other - distance * LANE).wait_send()

        @pl.when(place < deep - distance)
        def _():
            slot = me + distance * LANE
            sent(slot)
            for part in range(2):
                pl.when(place > 0)(lambda: downward(part, slot).wait_send())
                over(part, column_other + distance * LANE).wait_send()


def whole_rows(query, cur_kv, cur_pos, cache_kv, cache_pos, counts, visible):
    frames, tile_rows, columns, depth = query.shape
    queries = tile_rows * columns
    slots = cache_kv.shape[2]
    deep = lax.axis_size("tm") // LANE
    blocks = deep * LANE
    vmem = pl.BlockSpec(memory_space=pltpu.VMEM)
    smem = pl.BlockSpec(memory_space=pltpu.SMEM)
    hbm = pl.BlockSpec(memory_space=pltpu.HBM)
    output = pl.pallas_call(
        lambda *refs: span_kernel(deep, *refs),
        out_shape=jax.ShapeDtypeStruct((queries, depth), jnp.bfloat16),
        in_specs=[hbm, hbm, vmem, vmem, hbm, smem, smem],
        out_specs=vmem,
        scratch_shapes=[
            pltpu.VMEM((queries, depth), jnp.bfloat16),
            pltpu.VMEM((2, queries, depth), jnp.bfloat16),
            pltpu.VMEM((queries, depth), jnp.bfloat16),
            pltpu.VMEM((queries, depth), jnp.bfloat16),
            pltpu.VMEM((queries, HEAD), jnp.float32),
            pltpu.VMEM((queries, HEAD), jnp.float32),
            pltpu.VMEM((blocks, slots, depth + HEAD), jnp.bfloat16),
            pltpu.VMEM((blocks, slots, depth), jnp.bfloat16),
            pltpu.VMEM((3, 1, slots), jnp.int32),
            pltpu.VMEM((queries, depth), jnp.float32),
            pltpu.VMEM((queries, depth), jnp.float32),
            pltpu.VMEM((queries, depth), jnp.float32),
            pltpu.VMEM((16, LANE * slots), jnp.float32),
            pltpu.SemaphoreType.DMA((3,)),
            pltpu.SemaphoreType.DMA,
            pltpu.SemaphoreType.DMA((2, blocks, DIRECTIONS)),
            pltpu.SemaphoreType.DMA((2, blocks)),
        ],
        compiler_params=pltpu.CompilerParams(collective_id=0, has_side_effects=True),
    )(
        query.reshape(queries, depth),
        cur_kv.reshape(2, queries, depth),
        cur_pos.reshape(3, tile_rows, columns),
        cache_kv.reshape(2, slots, depth),
        jnp.transpose(cache_pos, (1, 0, 2)),
        counts,
        visible,
    )
    return output.reshape(frames, tile_rows, columns, depth)


def span_attention(query, *rest):
    fits = (
        lax.axis_size("height") == 1
        and query.shape[0] == 1
        and query.shape[1] <= REACH + 1
        and query.shape[1] * query.shape[2] % HEAD == 0
        and lax.axis_size("tm") % LANE == 0
    )
    return (whole_rows if fits else per_device)(query, *rest)


def solution(mesh):
    in_specs = (
        P(("group", "tm"), "height", None, None),
        P(None, ("group", "tm"), "height", None, None),
        P(None, ("group", "tm"), "height", None),
        P(("group", "tm"), None, "height", None),
        P(("group", "tm"), None, "height"),
        P(("group", "tm"), "height"),
        P(("group", "tm"), None),
    )
    out_specs = P(("group", "tm"), "height", None, None)
    return jax.shard_map(
        span_attention, mesh=mesh, in_specs=in_specs, out_specs=out_specs, check_vma=False
    )
```

```python
import jax
import jax.numpy as jnp
from jax import lax
from jax.experimental import pallas as pl
from jax.experimental.pallas import tpu as pltpu
from jax.sharding import PartitionSpec as P

HEADS = 12
HEAD = 128
REACH = 2


masked_value = -1e30


def extended(cells, sides, width):
    for axis, dim in sides:
        count = lax.axis_size(axis)
        ends = count - 1
        head = lax.slice_in_dim(cells, 0, width, axis=dim)
        tail = lax.slice_in_dim(cells, cells.shape[dim] - width, cells.shape[dim], axis=dim)
        cells = jnp.concatenate(
            [
                lax.ppermute(tail, axis, [(i, (i + 1) % count) for i in range(ends)]),
                cells,
                lax.ppermute(head, axis, [((i + 1) % count, i) for i in range(ends)]),
            ],
            axis=dim,
        )
    return cells


def rope_tables():
    half = HEAD // 2
    index = jnp.arange(half)
    first = HEAD // 8
    second = 3 * HEAD // 16
    member = (index >= first).astype(jnp.int32) + (index >= first + second).astype(jnp.int32)
    begin = jnp.where(member == 0, 0, jnp.where(member == 1, first, first + second))
    length = jnp.where(member == 0, first, jnp.where(member == 1, second, half - first - second))
    frequency = jnp.power(
        10000.0, -(index - begin).astype(jnp.float32) / length.astype(jnp.float32)
    )
    select = (member[None, :] == jnp.arange(3)[:, None]).astype(jnp.float32) * frequency[None, :]
    return select


def rotate(vectors, pos_time, pos_row, pos_column):
    select = rope_tables()
    angle = (
        pos_time.astype(jnp.float32)[..., None] * select[0]
        + pos_row.astype(jnp.float32)[..., None] * select[1]
        + pos_column.astype(jnp.float32)[..., None] * select[2]
    )
    cosine = jnp.cos(angle)[..., None, :]
    sine = jnp.sin(angle)[..., None, :]
    shaped = vectors.astype(jnp.float32).reshape(vectors.shape[:-1] + (HEADS, 2, HEAD // 2))
    lower = shaped[..., 0, :]
    upper = shaped[..., 1, :]
    turned = jnp.stack([lower * cosine - upper * sine, upper * cosine + lower * sine], axis=-2)
    return turned.reshape(vectors.shape).astype(jnp.bfloat16)


def per_device(query, cur_kv, cur_pos, cache_kv, cache_pos, counts, visible):
    frames, tile_rows, columns, depth = query.shape
    queries = tile_rows * columns
    scale = HEAD ** (-0.5)
    tile_index = lax.axis_index("height")
    frame_rows = tile_rows * lax.axis_size("height")
    q_rot = rotate(query, cur_pos[0], cur_pos[1], cur_pos[2]).reshape(frames, queries, HEADS, HEAD)
    q_heads = jnp.transpose(q_rot, (0, 2, 1, 3))
    k_rot = rotate(cur_kv[0], cur_pos[0], cur_pos[1], cur_pos[2])
    local_pair = jnp.stack([k_rot, cur_kv[1]])
    padded = extended(local_pair, (("height", 2),), REACH)
    extent = tile_rows + 2 * REACH
    local_keys = jnp.transpose(
        padded[0].reshape(frames, extent * columns, HEADS, HEAD), (0, 2, 1, 3)
    )
    local_values = jnp.transpose(
        padded[1].reshape(frames, extent * columns, HEADS, HEAD), (0, 2, 1, 3)
    )
    query_row = tile_index * tile_rows + jnp.arange(queries) // columns
    key_row = tile_index * tile_rows - REACH + jnp.arange(extent * columns) // columns
    local_ok = (
        (key_row[None, :] >= 0)
        & (key_row[None, :] < frame_rows)
        & (jnp.abs(query_row[:, None] - key_row[None, :]) <= REACH)
    )
    local_bias = jnp.where(local_ok, 0.0, masked_value).astype(jnp.float32)
    scores = (
        jnp.einsum("fhqd,fhkd->fhqk", q_heads, local_keys, preferred_element_type=jnp.float32)
        * scale
        + local_bias[None, None]
    )
    highest = jnp.max(scores, axis=-1)
    weights = jnp.exp(scores - highest[..., None])
    totals = jnp.sum(weights, axis=-1)
    summed = jnp.einsum(
        "fhqk,fhkd->fhqd",
        weights.astype(jnp.bfloat16),
        local_values,
        preferred_element_type=jnp.float32,
    )
    slots = cache_kv.shape[2]
    slot_index = jnp.arange(slots)
    pair_piece = lax.all_gather(cache_kv, "tm", axis=0, tiled=True)
    position_piece = lax.all_gather(cache_pos, "tm", axis=0, tiled=True)
    count_piece = lax.all_gather(counts, "tm", axis=0, tiled=True)
    turned = rotate(
        pair_piece[:, 0], position_piece[:, 0], position_piece[:, 1], position_piece[:, 2]
    )
    blocks = turned.shape[0]
    live = count_piece[:, 0]
    usable = (
        (visible[:, :, None] > 0) & (slot_index[None, None, :] < live[None, :, None])
    ).reshape(frames, blocks * slots)
    block_bias = jnp.where(usable, 0.0, masked_value).astype(jnp.float32)
    flat_keys = jnp.transpose(turned.reshape(blocks * slots, HEADS, HEAD), (1, 0, 2))
    flat_values = jnp.transpose(pair_piece[:, 1].reshape(blocks * slots, HEADS, HEAD), (1, 0, 2))
    block_scores = (
        jnp.einsum("fhqd,hkd->fhqk", q_heads, flat_keys, preferred_element_type=jnp.float32) * scale
        + block_bias[:, None, None, :]
    )
    new_max = jnp.maximum(highest, jnp.max(block_scores, axis=-1))
    block_weights = jnp.exp(block_scores - new_max[..., None])
    fading = jnp.exp(highest - new_max)
    added = jnp.einsum(
        "fhqk,hkd->fhqd",
        block_weights.astype(jnp.bfloat16),
        flat_values,
        preferred_element_type=jnp.float32,
    )
    final_total = totals * fading + jnp.sum(block_weights, axis=-1)
    final_sum = summed * fading[..., None] + added
    output = (final_sum / final_total[..., None]).astype(jnp.bfloat16)
    output = jnp.transpose(output, (0, 2, 1, 3))
    return output.reshape(frames, tile_rows, columns, depth)


CORES = 2
COLUMNS = 2
LANE = CORES * COLUMNS
DIRECTIONS = 4


def frequency_rows(axis, shape):
    half = HEAD // 2
    index = lax.broadcasted_iota(jnp.int32, shape, axis) % half
    first = HEAD // 8
    second = 3 * HEAD // 16
    member = (index >= first).astype(jnp.int32) + (index >= first + second).astype(jnp.int32)
    begin = jnp.where(member == 0, 0, jnp.where(member == 1, first, first + second))
    length = jnp.where(member == 0, first, jnp.where(member == 1, second, half - first - second))
    ratio = (index - begin).astype(jnp.float32) / length.astype(jnp.float32)
    return member, jnp.exp(-ratio * 9.210340371976184)


def turn_tables(pos_time, pos_row, pos_column):
    tokens = pos_time.shape[-1]
    member, _ = frequency_rows(0, (HEAD, tokens))
    chosen = jnp.where(member == 0, pos_time, jnp.where(member == 1, pos_row, pos_column))
    eye = (
        lax.broadcasted_iota(jnp.int32, (tokens, tokens), 0)
        == lax.broadcasted_iota(jnp.int32, (tokens, tokens), 1)
    ).astype(jnp.float32).astype(jnp.bfloat16)
    spread = lax.dot_general(
        eye,
        chosen.astype(jnp.float32).astype(jnp.bfloat16),
        (((1,), (1,)), ((), ())),
        preferred_element_type=jnp.float32,
    )
    _, frequency = frequency_rows(1, (1, HEAD))
    angle = spread * frequency
    lane = lax.broadcasted_iota(jnp.int32, (tokens, HEAD), 1)
    sine = jnp.sin(angle)
    return jnp.cos(angle), jnp.where(lane < HEAD // 2, -sine, sine)


def turn(vectors, cosine, sine):
    wide = vectors.astype(jnp.float32)
    return (wide * cosine + pltpu.roll(wide, HEAD // 2, 1) * sine).astype(jnp.bfloat16)


def fold(weights):
    pieces = [weights[:, i : i + HEAD] for i in range(0, weights.shape[1], HEAD)]
    return sum(pieces[1:], pieces[0])


def head_columns(h):
    return slice(h * HEAD, (h + 1) * HEAD)


def span_kernel(
    deep, q_hbm, kv_hbm, cur_pos_ref, cache_ref, cache_pos_hbm, count_ref, visible_ref, out_ref,
    q_raw, kv_raw, q_rot, k_rot, cos_ref, sin_ref, keys, values, kept_pos, top_ref, total_ref, sum_ref, bias_ref, load_sem, own_sem,
    send_sem, recv_sem,
):
    me = lax.axis_index("tm")
    place = me // LANE
    column = (me % LANE) // CORES
    core = me % CORES
    slots = cache_ref.shape[1]
    depth = cache_ref.shape[2]
    blocks = deep * LANE
    scale = HEAD ** (-0.5)
    core_other = me + 1 - 2 * core
    column_other = me + CORES - 2 * CORES * column
    barrier = pltpu.get_barrier_semaphore()

    def greet(device):
        pl.semaphore_signal(
            barrier, inc=1, device_id={"tm": device}, device_id_type=pl.DeviceIdType.MESH
        )

    load_pos = pltpu.make_async_copy(cache_pos_hbm, kept_pos, load_sem.at[2])
    load_pos.start()
    greet(core_other)
    greet(column_other)
    pl.when(place > 0)(lambda: greet(me - LANE))
    pl.when(place < deep - 1)(lambda: greet(me + LANE))

    load_q = pltpu.make_async_copy(q_hbm, q_raw, load_sem.at[0])
    load_kv = pltpu.make_async_copy(kv_hbm, kv_raw, load_sem.at[1])
    own_values = pltpu.make_async_copy(cache_ref.at[1], values.at[me], own_sem)
    load_q.start()
    load_kv.start()
    own_values.start()

    load_pos.wait()
    cosine, sine = turn_tables(kept_pos[0], kept_pos[1], kept_pos[2])
    for h in range(HEADS):
        keys[me, :, head_columns(h)] = turn(cache_ref[0, :, head_columns(h)], cosine, sine)
    row = lax.broadcasted_iota(jnp.int32, (slots, HEAD), 0)
    keys[me, :, depth:] = jnp.where(row < count_ref[0, 0], 0.0, masked_value).astype(jnp.bfloat16)

    pl.semaphore_wait(
        barrier,
        2 + (place > 0).astype(jnp.int32) + (place < deep - 1).astype(jnp.int32),
    )

    def message(part, slot, direction, device, own=False):
        buffer = (values, keys)[part]
        source = cache_ref.at[1] if own and part == 0 else buffer.at[slot]
        return pltpu.make_async_remote_copy(
            src_ref=source,
            dst_ref=buffer.at[slot],
            send_sem=send_sem.at[part, slot, direction],
            recv_sem=recv_sem.at[part, slot],
            device_id={"tm": device},
            device_id_type=pl.DeviceIdType.MESH,
        )

    def arrived(part, slot):
        message(part, slot, 0, core_other).wait_recv()

    def upward(part, slot, own=False):
        return message(part, slot, 0, me + LANE, own)

    def downward(part, slot, own=False):
        return message(part, slot, 1, me - LANE, own)

    def across(part, slot, own=False):
        return message(part, slot, 2, column_other, own)

    def over(part, slot, own=False):
        return message(part, slot, 3, core_other, own)

    for part in range(2):
        pl.when(place < deep - 1)(lambda: upward(part, me, True).start())
        pl.when(place > 0)(lambda: downward(part, me, True).start())
        across(part, me, True).start()
        over(part, me, True).start()

    def line(distance, part):
        @pl.when(place >= distance)
        def _():
            slot = me - distance * LANE
            arrived(part, slot)
            pl.when(place < deep - 1)(lambda: upward(part, slot).start())
            across(part, slot).start()
            over(part, slot).start()

        @pl.when(place < deep - distance)
        def _():
            slot = me + distance * LANE
            arrived(part, slot)
            pl.when(place > 0)(lambda: downward(part, slot).start())
            across(part, slot).start()
            over(part, slot).start()

    def side(distance, part):
        def relay(slot):
            arrived(part, slot)
            over(part, slot).start()

        if distance == 0:
            relay(column_other)
        else:
            pl.when(place >= distance)(lambda: relay(column_other - distance * LANE))
            pl.when(place < deep - distance)(lambda: relay(column_other + distance * LANE))

    load_q.wait()
    load_kv.wait()
    queries = q_raw.shape[0]
    span_rows = cur_pos_ref.shape[1]
    width = cur_pos_ref.shape[2]
    for r in range(span_rows):
        cosine, sine = turn_tables(
            cur_pos_ref[0, r : r + 1, :], cur_pos_ref[1, r : r + 1, :], cur_pos_ref[2, r : r + 1, :]
        )
        cos_ref[r * width : (r + 1) * width, :] = cosine
        sin_ref[r * width : (r + 1) * width, :] = sine

    def turn_current(first, last):
        for h in range(first, last):
            q_rot[:, head_columns(h)] = turn(q_raw[:, head_columns(h)], cos_ref[...], sin_ref[...])
            k_rot[:, head_columns(h)] = turn(
                kv_raw[0, :, head_columns(h)], cos_ref[...], sin_ref[...]
            )

    pick = (lax.broadcasted_iota(jnp.int32, (16, HEAD), 1) == 0).astype(jnp.float32)
    pick = pick.astype(jnp.bfloat16)
    transposed = (((1,), (1,)), ((), ()))
    def early_attention(numbers, start, stop):
        for h in range(start, stop):
            cols = head_columns(h)
            q = q_rot[:, cols]
            scores = [
                lax.dot_general(
                    q, k_rot[:, cols], transposed, preferred_element_type=jnp.float32
                ) * scale
            ]
            held = [kv_raw[1, :, cols]]
            for k, number in enumerate(numbers):
                part = pl.ds(number * LANE, LANE)
                block = keys[part, :, cols].reshape(LANE * slots, HEAD)
                scores.append(
                    lax.dot_general(q, block, transposed, preferred_element_type=jnp.float32)
                    * scale + bias_ref[16 * k : 16 * k + 1, :]
                )
                held.append(values[part, :, cols].reshape(LANE * slots, HEAD))
            highest = jnp.max(scores[0], axis=-1, keepdims=True)
            for score in scores[1:]:
                highest = jnp.maximum(highest, jnp.max(score, axis=-1, keepdims=True))
            weights = [jnp.exp(score - highest) for score in scores]
            top_ref[:, cols] = jnp.broadcast_to(highest, (queries, HEAD))
            total_ref[:, cols] = sum([fold(w) for w in weights[1:]], fold(weights[0]))
            products = [
                jnp.dot(w.astype(jnp.bfloat16), v, preferred_element_type=jnp.float32)
                for w, v in zip(weights, held)
            ]
            sum_ref[:, cols] = sum(products[1:], products[0])

    def gather(k, number):
        first = number * LANE
        for c in range(COLUMNS):
            for part in range(2):
                arrived(part, first + c * CORES + 1 - core)
        spans = []
        for i in range(LANE):
            seen = jnp.where(visible_ref[0, first + i] > 0, 0.0, masked_value)
            spans.append(
                jnp.minimum(keys[first + i, :, depth:].astype(jnp.float32), seen)
            )
        bias_ref[16 * k : 16 * (k + 1), :] = lax.dot_general(
            pick, jnp.concatenate(spans, axis=0).astype(jnp.bfloat16), transposed,
            preferred_element_type=jnp.float32,
        )

    def plane(k, number, start, stop, last):
        first = number * LANE
        bias = bias_ref[16 * k : 16 * k + 1, :]
        for h in range(start, stop):
            cols = head_columns(h)
            block = keys[pl.ds(first, LANE), :, cols].reshape(LANE * slots, HEAD)
            scores = lax.dot_general(
                q_rot[:, cols], block, transposed, preferred_element_type=jnp.float32
            ) * scale + bias
            old = top_ref[:, cols]
            highest = jnp.maximum(old, jnp.max(scores, axis=-1, keepdims=True))
            fading = jnp.exp(old - highest)
            weights = jnp.exp(scores - highest[:, 0:1])
            total = total_ref[:, cols] * fading + fold(weights)
            summed = sum_ref[:, cols] * fading + jnp.dot(
                weights.astype(jnp.bfloat16),
                values[pl.ds(first, LANE), :, cols].reshape(LANE * slots, HEAD),
                preferred_element_type=jnp.float32,
            )
            if last:
                out_ref[:, cols] = (
                    summed / jnp.sum(total, axis=-1, keepdims=True)
                ).astype(jnp.bfloat16)
            else:
                top_ref[:, cols] = highest
                total_ref[:, cols] = total
                sum_ref[:, cols] = summed

    nearest = [sorted(range(deep), key=lambda other: abs(other - z)) for z in range(deep)]

    def ordered(k):
        number = 0
        for z in range(deep):
            number = number + (place == z).astype(jnp.int32) * nearest[z][k]
        return number

    own_values.wait()
    half = HEADS // 2
    for distance in range(1, deep):
        for part in range(2):
            line(distance, part)
            side(distance - 1, part)
            if distance == 1:
                turn_current(part * half, HEADS if part else half)
    numbers = [ordered(k) for k in range(deep)]
    for k in range(deep - 1):
        gather(k, numbers[k])
    early_attention(numbers[:-1], 0, half)
    side(deep - 1, 0)
    early_attention(numbers[:-1], half, HEADS)
    side(deep - 1, 1)
    gather(deep - 1, numbers[-1])
    plane(deep - 1, numbers[-1], 0, HEADS, True)

    def sent(slot, own=False):
        for part in range(2):
            across(part, slot, own).wait_send()
            over(part, slot, own).wait_send()

    for part in range(2):
        pl.when(place < deep - 1)(lambda: upward(part, me, True).wait_send())
        pl.when(place > 0)(lambda: downward(part, me, True).wait_send())
    sent(me, True)
    for part in range(2):
        over(part, column_other).wait_send()
    for distance in range(1, deep):
        @pl.when(place >= distance)
        def _():
            slot = me - distance * LANE
            sent(slot)
            for part in range(2):
                pl.when(place < deep - 1)(lambda: upward(part, slot).wait_send())
                over(part, column_other - distance * LANE).wait_send()

        @pl.when(place < deep - distance)
        def _():
            slot = me + distance * LANE
            sent(slot)
            for part in range(2):
                pl.when(place > 0)(lambda: downward(part, slot).wait_send())
                over(part, column_other + distance * LANE).wait_send()


def whole_rows(query, cur_kv, cur_pos, cache_kv, cache_pos, counts, visible):
    frames, tile_rows, columns, depth = query.shape
    queries = tile_rows * columns
    slots = cache_kv.shape[2]
    deep = lax.axis_size("tm") // LANE
    blocks = deep * LANE
    vmem = pl.BlockSpec(memory_space=pltpu.VMEM)
    smem = pl.BlockSpec(memory_space=pltpu.SMEM)
    hbm = pl.BlockSpec(memory_space=pltpu.HBM)
    output = pl.pallas_call(
        lambda *refs: span_kernel(deep, *refs),
        out_shape=jax.ShapeDtypeStruct((queries, depth), jnp.bfloat16),
        in_specs=[hbm, hbm, vmem, vmem, hbm, smem, smem],
        out_specs=vmem,
        scratch_shapes=[
            pltpu.VMEM((queries, depth), jnp.bfloat16),
            pltpu.VMEM((2, queries, depth), jnp.bfloat16),
            pltpu.VMEM((queries, depth), jnp.bfloat16),
            pltpu.VMEM((queries, depth), jnp.bfloat16),
            pltpu.VMEM((queries, HEAD), jnp.float32),
            pltpu.VMEM((queries, HEAD), jnp.float32),
            pltpu.VMEM((blocks, slots, depth + HEAD), jnp.bfloat16),
            pltpu.VMEM((blocks, slots, depth), jnp.bfloat16),
            pltpu.VMEM((3, 1, slots), jnp.int32),
            pltpu.VMEM((queries, depth), jnp.float32),
            pltpu.VMEM((queries, depth), jnp.float32),
            pltpu.VMEM((queries, depth), jnp.float32),
            pltpu.VMEM((16 * deep, LANE * slots), jnp.float32),
            pltpu.SemaphoreType.DMA((3,)),
            pltpu.SemaphoreType.DMA,
            pltpu.SemaphoreType.DMA((2, blocks, DIRECTIONS)),
            pltpu.SemaphoreType.DMA((2, blocks)),
        ],
        compiler_params=pltpu.CompilerParams(collective_id=0, has_side_effects=True),
    )(
        query.reshape(queries, depth),
        cur_kv.reshape(2, queries, depth),
        cur_pos.reshape(3, tile_rows, columns),
        cache_kv.reshape(2, slots, depth),
        jnp.transpose(cache_pos, (1, 0, 2)),
        counts,
        visible,
    )
    return output.reshape(frames, tile_rows, columns, depth)


def span_attention(query, *rest):
    fits = (
        lax.axis_size("height") == 1
        and query.shape[0] == 1
        and query.shape[1] <= REACH + 1
        and query.shape[1] * query.shape[2] % HEAD == 0
        and lax.axis_size("tm") % LANE == 0
    )
    return (whole_rows if fits else per_device)(query, *rest)


def solution(mesh):
    in_specs = (
        P(("group", "tm"), "height", None, None),
        P(None, ("group", "tm"), "height", None, None),
        P(None, ("group", "tm"), "height", None),
        P(("group", "tm"), None, "height", None),
        P(("group", "tm"), None, "height"),
        P(("group", "tm"), "height"),
        P(("group", "tm"), None),
    )
    out_specs = P(("group", "tm"), "height", None, None)
    return jax.shard_map(
        span_attention, mesh=mesh, in_specs=in_specs, out_specs=out_specs, check_vma=False
    )
```

```python
import jax
import jax.numpy as jnp
from jax import lax
from jax.experimental import pallas as pl
from jax.experimental.pallas import tpu as pltpu
from jax.sharding import PartitionSpec as P

HEADS = 12
HEAD = 128
REACH = 2


masked_value = -1e30


def extended(cells, sides, width):
    for axis, dim in sides:
        count = lax.axis_size(axis)
        ends = count - 1
        head = lax.slice_in_dim(cells, 0, width, axis=dim)
        tail = lax.slice_in_dim(cells, cells.shape[dim] - width, cells.shape[dim], axis=dim)
        cells = jnp.concatenate(
            [
                lax.ppermute(tail, axis, [(i, (i + 1) % count) for i in range(ends)]),
                cells,
                lax.ppermute(head, axis, [((i + 1) % count, i) for i in range(ends)]),
            ],
            axis=dim,
        )
    return cells


def rope_tables():
    half = HEAD // 2
    index = jnp.arange(half)
    first = HEAD // 8
    second = 3 * HEAD // 16
    member = (index >= first).astype(jnp.int32) + (index >= first + second).astype(jnp.int32)
    begin = jnp.where(member == 0, 0, jnp.where(member == 1, first, first + second))
    length = jnp.where(member == 0, first, jnp.where(member == 1, second, half - first - second))
    frequency = jnp.power(
        10000.0, -(index - begin).astype(jnp.float32) / length.astype(jnp.float32)
    )
    select = (member[None, :] == jnp.arange(3)[:, None]).astype(jnp.float32) * frequency[None, :]
    return select


def rotate(vectors, pos_time, pos_row, pos_column):
    select = rope_tables()
    angle = (
        pos_time.astype(jnp.float32)[..., None] * select[0]
        + pos_row.astype(jnp.float32)[..., None] * select[1]
        + pos_column.astype(jnp.float32)[..., None] * select[2]
    )
    cosine = jnp.cos(angle)[..., None, :]
    sine = jnp.sin(angle)[..., None, :]
    shaped = vectors.astype(jnp.float32).reshape(vectors.shape[:-1] + (HEADS, 2, HEAD // 2))
    lower = shaped[..., 0, :]
    upper = shaped[..., 1, :]
    turned = jnp.stack([lower * cosine - upper * sine, upper * cosine + lower * sine], axis=-2)
    return turned.reshape(vectors.shape).astype(jnp.bfloat16)


def per_device(query, cur_kv, cur_pos, cache_kv, cache_pos, counts, visible):
    frames, tile_rows, columns, depth = query.shape
    queries = tile_rows * columns
    scale = HEAD ** (-0.5)
    tile_index = lax.axis_index("height")
    frame_rows = tile_rows * lax.axis_size("height")
    q_rot = rotate(query, cur_pos[0], cur_pos[1], cur_pos[2]).reshape(frames, queries, HEADS, HEAD)
    q_heads = jnp.transpose(q_rot, (0, 2, 1, 3))
    k_rot = rotate(cur_kv[0], cur_pos[0], cur_pos[1], cur_pos[2])
    local_pair = jnp.stack([k_rot, cur_kv[1]])
    padded = extended(local_pair, (("height", 2),), REACH)
    extent = tile_rows + 2 * REACH
    local_keys = jnp.transpose(
        padded[0].reshape(frames, extent * columns, HEADS, HEAD), (0, 2, 1, 3)
    )
    local_values = jnp.transpose(
        padded[1].reshape(frames, extent * columns, HEADS, HEAD), (0, 2, 1, 3)
    )
    query_row = tile_index * tile_rows + jnp.arange(queries) // columns
    key_row = tile_index * tile_rows - REACH + jnp.arange(extent * columns) // columns
    local_ok = (
        (key_row[None, :] >= 0)
        & (key_row[None, :] < frame_rows)
        & (jnp.abs(query_row[:, None] - key_row[None, :]) <= REACH)
    )
    local_bias = jnp.where(local_ok, 0.0, masked_value).astype(jnp.float32)
    scores = (
        jnp.einsum("fhqd,fhkd->fhqk", q_heads, local_keys, preferred_element_type=jnp.float32)
        * scale
        + local_bias[None, None]
    )
    highest = jnp.max(scores, axis=-1)
    weights = jnp.exp(scores - highest[..., None])
    totals = jnp.sum(weights, axis=-1)
    summed = jnp.einsum(
        "fhqk,fhkd->fhqd",
        weights.astype(jnp.bfloat16),
        local_values,
        preferred_element_type=jnp.float32,
    )
    slots = cache_kv.shape[2]
    slot_index = jnp.arange(slots)
    pair_piece = lax.all_gather(cache_kv, "tm", axis=0, tiled=True)
    position_piece = lax.all_gather(cache_pos, "tm", axis=0, tiled=True)
    count_piece = lax.all_gather(counts, "tm", axis=0, tiled=True)
    turned = rotate(
        pair_piece[:, 0], position_piece[:, 0], position_piece[:, 1], position_piece[:, 2]
    )
    blocks = turned.shape[0]
    live = count_piece[:, 0]
    usable = (
        (visible[:, :, None] > 0) & (slot_index[None, None, :] < live[None, :, None])
    ).reshape(frames, blocks * slots)
    block_bias = jnp.where(usable, 0.0, masked_value).astype(jnp.float32)
    flat_keys = jnp.transpose(turned.reshape(blocks * slots, HEADS, HEAD), (1, 0, 2))
    flat_values = jnp.transpose(pair_piece[:, 1].reshape(blocks * slots, HEADS, HEAD), (1, 0, 2))
    block_scores = (
        jnp.einsum("fhqd,hkd->fhqk", q_heads, flat_keys, preferred_element_type=jnp.float32) * scale
        + block_bias[:, None, None, :]
    )
    new_max = jnp.maximum(highest, jnp.max(block_scores, axis=-1))
    block_weights = jnp.exp(block_scores - new_max[..., None])
    fading = jnp.exp(highest - new_max)
    added = jnp.einsum(
        "fhqk,hkd->fhqd",
        block_weights.astype(jnp.bfloat16),
        flat_values,
        preferred_element_type=jnp.float32,
    )
    final_total = totals * fading + jnp.sum(block_weights, axis=-1)
    final_sum = summed * fading[..., None] + added
    output = (final_sum / final_total[..., None]).astype(jnp.bfloat16)
    output = jnp.transpose(output, (0, 2, 1, 3))
    return output.reshape(frames, tile_rows, columns, depth)


CORES = 2
COLUMNS = 2
LANE = CORES * COLUMNS
DIRECTIONS = 4


def frequency_rows(axis, shape):
    half = HEAD // 2
    index = lax.broadcasted_iota(jnp.int32, shape, axis) % half
    first = HEAD // 8
    second = 3 * HEAD // 16
    member = (index >= first).astype(jnp.int32) + (index >= first + second).astype(jnp.int32)
    begin = jnp.where(member == 0, 0, jnp.where(member == 1, first, first + second))
    length = jnp.where(member == 0, first, jnp.where(member == 1, second, half - first - second))
    ratio = (index - begin).astype(jnp.float32) / length.astype(jnp.float32)
    return member, jnp.exp(-ratio * 9.210340371976184)


def turn_tables(pos_time, pos_row, pos_column):
    tokens = pos_time.shape[-1]
    member, _ = frequency_rows(0, (HEAD, tokens))
    chosen = jnp.where(member == 0, pos_time, jnp.where(member == 1, pos_row, pos_column))
    eye = (
        lax.broadcasted_iota(jnp.int32, (tokens, tokens), 0)
        == lax.broadcasted_iota(jnp.int32, (tokens, tokens), 1)
    ).astype(jnp.float32).astype(jnp.bfloat16)
    spread = lax.dot_general(
        eye,
        chosen.astype(jnp.float32).astype(jnp.bfloat16),
        (((1,), (1,)), ((), ())),
        preferred_element_type=jnp.float32,
    )
    _, frequency = frequency_rows(1, (1, HEAD))
    angle = spread * frequency
    lane = lax.broadcasted_iota(jnp.int32, (tokens, HEAD), 1)
    sine = jnp.sin(angle)
    return jnp.cos(angle), jnp.where(lane < HEAD // 2, -sine, sine)


def turn(vectors, cosine, sine):
    wide = vectors.astype(jnp.float32)
    return (wide * cosine + pltpu.roll(wide, HEAD // 2, 1) * sine).astype(jnp.bfloat16)


def head_columns(h):
    return slice(h * HEAD, (h + 1) * HEAD)


def span_kernel(
    deep, q_hbm, kv_hbm, cur_pos_ref, cache_ref, cache_pos_hbm, count_ref, visible_ref, out_ref,
    q_raw, kv_raw, q_rot, k_rot, cos_ref, sin_ref, keys, values, bias_ref, kept_pos, load_sem, own_sem,
    send_sem, recv_sem,
):
    me = lax.axis_index("tm")
    place = me // LANE
    column = (me % LANE) // CORES
    core = me % CORES
    slots = cache_ref.shape[1]
    depth = cache_ref.shape[2]
    blocks = deep * LANE
    scale = HEAD ** (-0.5)
    core_other = me + 1 - 2 * core
    column_other = me + CORES - 2 * CORES * column
    barrier = pltpu.get_barrier_semaphore()

    def greet(device):
        pl.semaphore_signal(
            barrier, inc=1, device_id={"tm": device}, device_id_type=pl.DeviceIdType.MESH
        )

    load_pos = pltpu.make_async_copy(cache_pos_hbm, kept_pos, load_sem.at[2])
    load_pos.start()
    greet(core_other)
    greet(column_other)
    pl.when(place > 0)(lambda: greet(me - LANE))
    pl.when(place < deep - 1)(lambda: greet(me + LANE))

    load_q = pltpu.make_async_copy(q_hbm, q_raw, load_sem.at[0])
    load_kv = pltpu.make_async_copy(kv_hbm, kv_raw, load_sem.at[1])
    own_values = pltpu.make_async_copy(cache_ref.at[1], values.at[me], own_sem)
    load_q.start()
    load_kv.start()
    own_values.start()

    load_pos.wait()
    cosine, sine = turn_tables(kept_pos[0], kept_pos[1], kept_pos[2])
    for h in range(HEADS):
        keys[me, :, head_columns(h)] = turn(cache_ref[0, :, head_columns(h)], cosine, sine)
    row = lax.broadcasted_iota(jnp.int32, (slots, HEAD), 0)
    keys[me, :, depth:] = jnp.where(row < count_ref[0, 0], 0.0, masked_value).astype(jnp.bfloat16)

    pl.semaphore_wait(
        barrier,
        2 + (place > 0).astype(jnp.int32) + (place < deep - 1).astype(jnp.int32),
    )

    def message(part, slot, direction, device, own=False):
        buffer = (values, keys)[part]
        source = cache_ref.at[1] if own and part == 0 else buffer.at[slot]
        return pltpu.make_async_remote_copy(
            src_ref=source,
            dst_ref=buffer.at[slot],
            send_sem=send_sem.at[part, slot, direction],
            recv_sem=recv_sem.at[part, slot],
            device_id={"tm": device},
            device_id_type=pl.DeviceIdType.MESH,
        )

    def arrived(part, slot):
        message(part, slot, 0, core_other).wait_recv()

    def upward(part, slot, own=False):
        return message(part, slot, 0, me + LANE, own)

    def downward(part, slot, own=False):
        return message(part, slot, 1, me - LANE, own)

    def across(part, slot, own=False):
        return message(part, slot, 2, column_other, own)

    def over(part, slot, own=False):
        return message(part, slot, 3, core_other, own)

    for part in range(2):
        pl.when(place < deep - 1)(lambda: upward(part, me, True).start())
        pl.when(place > 0)(lambda: downward(part, me, True).start())
        across(part, me, True).start()
        over(part, me, True).start()

    def line(distance, part):
        @pl.when(place >= distance)
        def _():
            slot = me - distance * LANE
            arrived(part, slot)
            pl.when(place < deep - 1)(lambda: upward(part, slot).start())
            across(part, slot).start()
            over(part, slot).start()

        @pl.when(place < deep - distance)
        def _():
            slot = me + distance * LANE
            arrived(part, slot)
            pl.when(place > 0)(lambda: downward(part, slot).start())
            across(part, slot).start()
            over(part, slot).start()

    def side(distance, part):
        def relay(slot):
            arrived(part, slot)
            over(part, slot).start()

        if distance == 0:
            relay(column_other)
        else:
            pl.when(place >= distance)(lambda: relay(column_other - distance * LANE))
            pl.when(place < deep - distance)(lambda: relay(column_other + distance * LANE))

    for distance in range(1, deep):
        for part in range(2):
            line(distance, part)
            side(distance - 1, part)
    load_q.wait()
    load_kv.wait()
    queries = q_raw.shape[0]
    span_rows = cur_pos_ref.shape[1]
    width = cur_pos_ref.shape[2]
    for r in range(span_rows):
        cosine, sine = turn_tables(
            cur_pos_ref[0, r : r + 1, :], cur_pos_ref[1, r : r + 1, :], cur_pos_ref[2, r : r + 1, :]
        )
        cos_ref[r * width : (r + 1) * width, :] = cosine
        sin_ref[r * width : (r + 1) * width, :] = sine

    def turn_current(first, last):
        for h in range(first, last):
            q_rot[:, head_columns(h)] = turn(q_raw[:, head_columns(h)], cos_ref[...], sin_ref[...])
            k_rot[:, head_columns(h)] = turn(
                kv_raw[0, :, head_columns(h)], cos_ref[...], sin_ref[...]
            )

    turn_current(0, HEADS)
    for part in range(2):
        side(deep - 1, part)
    for far in range(deep):
        for c in range(COLUMNS):
            for part in range(2):
                arrived(part, far * LANE + c * CORES + 1 - core)
    own_values.wait()

    for e in range(blocks):
        seen = jnp.where(visible_ref[0, e] > 0, 0.0, masked_value)
        bias_ref[e * slots : (e + 1) * slots, :] = jnp.minimum(
            keys[e, :, depth:].astype(jnp.float32), seen
        ).astype(jnp.bfloat16)
    pick = (lax.broadcasted_iota(jnp.int32, (16, HEAD), 1) == 0).astype(jnp.float32)
    bias = lax.dot_general(
        pick.astype(jnp.bfloat16), bias_ref[...], (((1,), (1,)), ((), ())),
        preferred_element_type=jnp.float32,
    )[0:1, :]
    for h in range(HEADS):
        cols = head_columns(h)
        q = q_rot[:, cols]
        near = lax.dot_general(
            q, k_rot[:, cols], (((1,), (1,)), ((), ())), preferred_element_type=jnp.float32
        ) * scale
        far = lax.dot_general(
            q, keys[:, :, cols].reshape(blocks * slots, HEAD), (((1,), (1,)), ((), ())),
            preferred_element_type=jnp.float32,
        ) * scale + bias
        highest = jnp.maximum(
            jnp.max(near, axis=-1, keepdims=True), jnp.max(far, axis=-1, keepdims=True)
        )
        near = jnp.exp(near - highest)
        far = jnp.exp(far - highest)
        total = jnp.sum(near, axis=-1, keepdims=True) + jnp.sum(far, axis=-1, keepdims=True)
        summed = jnp.dot(
            near.astype(jnp.bfloat16), kv_raw[1, :, cols], preferred_element_type=jnp.float32
        ) + jnp.dot(
            far.astype(jnp.bfloat16), values[:, :, cols].reshape(blocks * slots, HEAD),
            preferred_element_type=jnp.float32,
        )
        out_ref[:, cols] = (summed / total).astype(jnp.bfloat16)

    def sent(slot, own=False):
        for part in range(2):
            across(part, slot, own).wait_send()
            over(part, slot, own).wait_send()

    for part in range(2):
        pl.when(place < deep - 1)(lambda: upward(part, me, True).wait_send())
        pl.when(place > 0)(lambda: downward(part, me, True).wait_send())
    sent(me, True)
    for part in range(2):
        over(part, column_other).wait_send()
    for distance in range(1, deep):
        @pl.when(place >= distance)
        def _():
            slot = me - distance * LANE
            sent(slot)
            for part in range(2):
                pl.when(place < deep - 1)(lambda: upward(part, slot).wait_send())
                over(part, column_other - distance * LANE).wait_send()

        @pl.when(place < deep - distance)
        def _():
            slot = me + distance * LANE
            sent(slot)
            for part in range(2):
                pl.when(place > 0)(lambda: downward(part, slot).wait_send())
                over(part, column_other + distance * LANE).wait_send()


def whole_rows(query, cur_kv, cur_pos, cache_kv, cache_pos, counts, visible):
    frames, tile_rows, columns, depth = query.shape
    queries = tile_rows * columns
    slots = cache_kv.shape[2]
    deep = lax.axis_size("tm") // LANE
    blocks = deep * LANE
    vmem = pl.BlockSpec(memory_space=pltpu.VMEM)
    smem = pl.BlockSpec(memory_space=pltpu.SMEM)
    hbm = pl.BlockSpec(memory_space=pl.ANY)
    output = pl.pallas_call(
        lambda *refs: span_kernel(deep, *refs),
        out_shape=jax.ShapeDtypeStruct((queries, depth), jnp.bfloat16),
        in_specs=[hbm, hbm, vmem, vmem, hbm, smem, smem],
        out_specs=vmem,
        scratch_shapes=[
            pltpu.VMEM((queries, depth), jnp.bfloat16),
            pltpu.VMEM((2, queries, depth), jnp.bfloat16),
            pltpu.VMEM((queries, depth), jnp.bfloat16),
            pltpu.VMEM((queries, depth), jnp.bfloat16),
            pltpu.VMEM((queries, HEAD), jnp.float32),
            pltpu.VMEM((queries, HEAD), jnp.float32),
            pltpu.VMEM((blocks, slots, depth + HEAD), jnp.bfloat16),
            pltpu.VMEM((blocks, slots, depth), jnp.bfloat16),
            pltpu.VMEM((blocks * slots, HEAD), jnp.bfloat16),
            pltpu.VMEM((3, 1, slots), jnp.int32),
            pltpu.SemaphoreType.DMA((3,)),
            pltpu.SemaphoreType.DMA,
            pltpu.SemaphoreType.DMA((2, blocks, DIRECTIONS)),
            pltpu.SemaphoreType.DMA((2, blocks)),
        ],
        compiler_params=pltpu.CompilerParams(collective_id=0, has_side_effects=True),
    )(
        query.reshape(queries, depth),
        cur_kv.reshape(2, queries, depth),
        cur_pos.reshape(3, tile_rows, columns),
        cache_kv.reshape(2, slots, depth),
        jnp.transpose(cache_pos, (1, 0, 2)),
        counts,
        visible,
    )
    return output.reshape(frames, tile_rows, columns, depth)


def span_attention(query, *rest):
    fits = (
        lax.axis_size("height") == 1
        and query.shape[0] == 1
        and query.shape[1] <= REACH + 1
        and lax.axis_size("tm") % LANE == 0
    )
    return (whole_rows if fits else per_device)(query, *rest)


def solution(mesh):
    in_specs = (
        P(("group", "tm"), "height", None, None),
        P(None, ("group", "tm"), "height", None, None),
        P(None, ("group", "tm"), "height", None),
        P(("group", "tm"), None, "height", None),
        P(("group", "tm"), None, "height"),
        P(("group", "tm"), "height"),
        P(("group", "tm"), None),
    )
    out_specs = P(("group", "tm"), "height", None, None)
    return jax.shard_map(
        span_attention, mesh=mesh, in_specs=in_specs, out_specs=out_specs, check_vma=False
    )
```
